32 devices in a mesh: rows: 8 (over z, y), grp: 4 (over x, core).
Axes of the slice: x: 2, y: 2, z: 4, core: 2. Of those that a mesh axis runs over, the one named last changes fastest.
Arguments:
- features: bfloat16 [4096, 512], P(('rows', 'grp')), may hold values from -6 to 6
- tile_entries: bfloat16 [64, 64, 1024], P(('rows', 'grp'))
- tile_columns: int32 [64, 16], P(('rows', 'grp')), may hold values from 0 to 63, as said below
- tiles_per_row: int32 [64], P(('rows', 'grp')), may hold values from 1 to 16, as said below
- rev_vals: bfloat16 [64, 64, 1024], P(('rows', 'grp'))
- rev_cols: int32 [64, 16], P(('rows', 'grp')), may hold values from 0 to 63, as said below
- rev_count: int32 [64], P(('rows', 'grp')), may hold values from 1 to 16, as said below
- w_first: bfloat16 [512, 512], replicated, may hold values from -0.25 to 0.25
- w_second: bfloat16 [512, 512], replicated, may hold values from -0.25 to 0.25
- cotangent: bfloat16 [4096, 512], P(('rows', 'grp')), may hold values from -0.09375 to 0.09375
Outputs:
- z_out: bfloat16 [4096, 512], P(('rows', 'grp'))
- grad_first: float32 [512, 512], replicated
- grad_second: float32 [512, 512], replicated
The draws below stay inside these ranges and needn't reach their ends.
Inputs may be any that keep to these rules, and one draw needn't show every extreme that they name: `tile_columns`: within each block row the 16 slots name distinct block columns; for each slot s, the block columns named in slot s over all block rows are all different. `tiles_per_row`: some block row has exactly 16 tiles. `rev_cols`: within each block column the slots name distinct block rows; the live transposed slots of block column c hold exactly the transposes of the live tiles of A in block column c. `rev_count`: some block column has exactly 16 tiles.
All inputs are finite; a program needn't handle non-finite values.
Results may differ from the reference program's by a relative error of at most 0.0062.
Values may be sent and summed in bfloat16 or wider, within the bound.
No kernel may reach another device: no remote copies, remote signals or barrier semaphores. Data moves between devices by JAX's collectives and lax.ppermute only.
A program may use at most 128 MiB of HBM per device.

```python
import jax
import jax.numpy as jnp
from jax import lax

HID = 512
BLK = 64
MOST = 16
NB = 64
NODES = 4096


def pattern(key):
    sigma = jax.random.permutation(jax.random.fold_in(key, 11), NB).astype(jnp.int32)
    tau = jax.random.permutation(jax.random.fold_in(key, 12), NB).astype(jnp.int32)
    offsets = jax.random.permutation(jax.random.fold_in(key, 13), NB)[:MOST].astype(jnp.int32)
    sigma_inv = jnp.argsort(sigma).astype(jnp.int32)
    tau_inv = jnp.argsort(tau).astype(jnp.int32)
    columns = sigma[(tau[:, None] + offsets[None, :]) % NB]
    sources = tau_inv[(sigma_inv[:, None] - offsets[None, :] + NB) % NB]
    block_ids = lax.broadcasted_iota(jnp.int32, (NB,), 0)
    counts = jax.random.randint(jax.random.fold_in(key, 1), (NB,), 1, MOST + 1)
    fullest = jax.random.randint(jax.random.fold_in(key, 2), (), 0, NB)
    full_column = jax.random.randint(jax.random.fold_in(key, 3), (), 0, NB)
    full_rows = sources[full_column]
    forced = jnp.any(block_ids[:, None] == full_rows[None, :], axis=1) | (block_ids == fullest)
    counts = jnp.where(forced, MOST, counts).astype(jnp.int32)
    slot_ids = lax.broadcasted_iota(jnp.int32, (NB, MOST), 1)
    live_rev = (slot_ids < counts[sources]).astype(jnp.int32)
    order = jnp.argsort(1 - live_rev, axis=1, stable=True).astype(jnp.int32)
    rev_cols = jnp.take_along_axis(sources, order, axis=1).astype(jnp.int32)
    rev_count = jnp.sum(live_rev, axis=1).astype(jnp.int32)
    return (columns.astype(jnp.int32), counts, order, rev_cols, rev_count)


def tile_base(key):
    scale = (BLK * MOST // 2) ** (-0.5)
    base_key = jax.random.fold_in(key, 21)
    values = jax.random.normal(base_key, (NB, MOST, BLK, BLK), jnp.float32)
    return values * scale


def draw_tile_columns(key, part):
    return pattern(key)[0]


def draw_tiles_per_row(key, part):
    return pattern(key)[1]


def draw_rev_cols(key, part):
    return pattern(key)[3]


def draw_rev_count(key, part):
    return pattern(key)[4]


def draw_tile_entries(key, part):
    base = tile_base(key)
    return base.transpose(0, 2, 1, 3).reshape(NB, BLK, MOST * BLK).astype(jnp.bfloat16)


def draw_rev_vals(key, part):
    base = tile_base(key)
    columns, counts, order, rev_cols, rev_count = pattern(key)
    picked = base[rev_cols, order]
    return picked.transpose(0, 3, 1, 2).reshape(NB, BLK, MOST * BLK).astype(jnp.bfloat16)


def levels(own_key, shape, shards, low, high):
    level, own = 1.0, jax.random.fold_in(own_key, 6)
    for position, blocks in shards:
        steps = jnp.exp(jax.random.uniform(jax.random.fold_in(own, position), (blocks,), jnp.float32, low / len(shards), high / len(shards)))
        level = level * jnp.repeat(steps, shape[position] // blocks).reshape([-1 if axis == position else 1 for axis in range(len(shape))])
    return level


def bell_draw(stream_key, shape, width, limit, cuts=(), kind=jnp.bfloat16):
    loudness = levels(stream_key, shape, cuts, -0.22, 0.18) if cuts else 1.0
    array = jax.random.normal(stream_key, shape, jnp.float32) * width * loudness
    return jnp.minimum(jnp.maximum(array, -limit), limit).astype(kind)


def setup_inputs(seed: int = 0) -> dict:
    key_of = jax.random.split(jax.random.key(seed), 11)
    return {
        "features": bell_draw(key_of[0], (NODES, HID), 1.0, 6.0, ((0, 32),)),
        "tile_entries": draw_tile_entries(jax.random.fold_in(key_of[10], 71), 0),
        "tile_columns": draw_tile_columns(jax.random.fold_in(key_of[10], 71), 0),
        "tiles_per_row": draw_tiles_per_row(jax.random.fold_in(key_of[10], 71), 0),
        "rev_vals": draw_rev_vals(jax.random.fold_in(key_of[10], 71), 0),
        "rev_cols": draw_rev_cols(jax.random.fold_in(key_of[10], 71), 0),
        "rev_count": draw_rev_count(jax.random.fold_in(key_of[10], 71), 0),
        "w_first": bell_draw(key_of[7], (HID, HID), HID ** -0.5, 0.25),
        "w_second": bell_draw(key_of[8], (HID, HID), HID ** -0.5, 0.25),
        "cotangent": bell_draw(key_of[9], (NODES, HID), NODES ** -0.5, 0.09375, ((0, 32),)),
    }


def active_slots(tile_columns, tiles_per_row):
    return lax.broadcasted_iota(jnp.int32, tile_columns.shape, 1) < tiles_per_row[:, None]


def aggregate(vertex_rows, tile_entries, tile_columns, tiles_per_row):
    channels = vertex_rows.shape[1]
    block_table = vertex_rows.reshape(NB, BLK, channels)
    slot_active = active_slots(tile_columns, tiles_per_row).astype(vertex_rows.dtype)

    def single_row(packed):
        panel_row, columns, weights = packed
        picked = (block_table[columns] * weights[:, None, None]).reshape(MOST * BLK, channels)
        return jnp.dot(panel_row, picked, preferred_element_type=jnp.float32)

    summed_rows = lax.map(single_row, (tile_entries, tile_columns, slot_active))
    return summed_rows.reshape(NODES, channels) + vertex_rows.astype(jnp.float32)


def silu_slope(values):
    sigmoid_part = jax.nn.sigmoid(values)
    return sigmoid_part * (1.0 + values * (1.0 - sigmoid_part))


def reference(features, tile_entries, tile_columns, tiles_per_row, rev_vals, rev_cols, rev_count, w_first, w_second, cotangent):
    mixed_first = aggregate(features, tile_entries, tile_columns, tiles_per_row).astype(jnp.bfloat16)
    pre_first = jnp.dot(mixed_first, w_first, preferred_element_type=jnp.float32)
    hidden = jax.nn.silu(pre_first).astype(jnp.bfloat16)
    mixed_second = aggregate(hidden, tile_entries, tile_columns, tiles_per_row).astype(jnp.bfloat16)
    z_out = jnp.dot(mixed_second, w_second, preferred_element_type=jnp.float32).astype(jnp.bfloat16)
    grad_second = jnp.dot(mixed_second.T, cotangent, preferred_element_type=jnp.float32)
    back_second = jnp.dot(cotangent, w_second.T, preferred_element_type=jnp.float32).astype(jnp.bfloat16)
    back_hidden = aggregate(back_second, rev_vals, rev_cols, rev_count)
    back_first = (back_hidden * silu_slope(pre_first)).astype(jnp.bfloat16)
    grad_first = jnp.dot(mixed_first.T, back_first, preferred_element_type=jnp.float32)
    return z_out, grad_first, grad_second
```

```python
import jax
import jax.numpy as jnp
from jax import lax
from jax.sharding import PartitionSpec as P

AXES = ("rows", "grp")


def aggregate(panel_vals, strip_columns, strip_count, everyone, own_rows):
    blocks, size_block, span_width = panel_vals.shape
    slot_count = span_width // size_block
    channels = everyone.shape[1]
    block_table = everyone.reshape(-1, size_block, channels)
    slot_ids = lax.broadcasted_iota(jnp.int32, strip_columns.shape, 1)
    weights = (slot_ids < strip_count[:, None]).astype(everyone.dtype)
    picked = (block_table[strip_columns] * weights[:, :, None, None]).reshape(
        blocks, slot_count * size_block, channels
    )
    summed_rows = jnp.einsum("bik,bkc->bic", panel_vals, picked, preferred_element_type=jnp.float32)
    return summed_rows.reshape(blocks * size_block, channels) + own_rows.astype(jnp.float32)


def shards(
    features,
    tile_entries,
    tile_columns,
    tiles_per_row,
    rev_vals,
    rev_cols,
    rev_count,
    w_first,
    w_second,
    cotangent,
):
    f32, bf16 = jnp.float32, jnp.bfloat16
    channels = features.shape[1]
    pair = jnp.concatenate([features, cotangent], axis=1)
    pair_all = lax.all_gather(pair, AXES, axis=0, tiled=True)
    mixed_own = aggregate(
        tile_entries, tile_columns, tiles_per_row, pair_all[:, :channels], features
    ).astype(bf16)
    spread_own = aggregate(
        rev_vals, rev_cols, rev_count, pair_all[:, channels:], cotangent
    ).astype(bf16)
    both_all = lax.all_gather(
        jnp.concatenate([mixed_own, spread_own], axis=1), AXES, axis=0, tiled=True
    )
    mixed = both_all[:, :channels]
    spread = both_all[:, channels:]
    pre_first = jnp.dot(mixed, w_first, preferred_element_type=f32)
    sig = jax.nn.sigmoid(pre_first)
    hidden = (pre_first * sig).astype(bf16)
    slope = sig * (1.0 + pre_first * (1.0 - sig))
    back_hidden = lax.dot_general(
        spread, w_second, (((1,), (1,)), ((), ())), preferred_element_type=f32
    )
    back_first = (back_hidden * slope).astype(bf16)
    grad_first = lax.dot_general(
        mixed, back_first, (((0,), (0,)), ((), ())), preferred_element_type=f32
    )
    grad_second = lax.dot_general(
        hidden, spread, (((0,), (0,)), ((), ())), preferred_element_type=f32
    )
    position = lax.axis_index(AXES) * features.shape[0]
    hidden_own = lax.dynamic_slice_in_dim(hidden, position, features.shape[0], 0)
    mixed_second = aggregate(
        tile_entries, tile_columns, tiles_per_row, hidden, hidden_own
    ).astype(bf16)
    z_out = jnp.dot(mixed_second, w_second, preferred_element_type=f32).astype(bf16)
    return (z_out, grad_first, grad_second)


def solution(mesh):
    placed = (
        P(AXES, None),
        P(AXES, None, None),
        P(AXES, None),
        P(AXES),
        P(AXES, None, None),
        P(AXES, None),
        P(AXES),
        P(),
        P(),
        P(AXES, None),
    )
    return jax.shard_map(
        shards,
        mesh=mesh,
        in_specs=placed,
        out_specs=(P(AXES, None), P(), P()),
        check_vma=False,
    )
```

```python
import jax
import jax.numpy as jnp
from jax import lax
from jax.experimental import pallas as pl
from jax.experimental.pallas import tpu as pltpu
from jax.sharding import PartitionSpec as P

AXES = ("rows", "grp")
F32 = jnp.float32
BF16 = jnp.bfloat16


def aggregate(panel_vals, strip_columns, strip_count, everyone, own_rows):
    blocks, size_block, span_width = panel_vals.shape
    slot_count = span_width // size_block
    channels = everyone.shape[1]
    block_table = everyone.reshape(-1, size_block, channels)
    slot_ids = lax.broadcasted_iota(jnp.int32, strip_columns.shape, 1)
    weights = (slot_ids < strip_count[:, None]).astype(everyone.dtype)
    picked = (block_table[strip_columns] * weights[:, :, None, None]).reshape(
        blocks, slot_count * size_block, channels
    )
    summed_rows = jnp.einsum("bik,bkc->bic", panel_vals, picked, preferred_element_type=F32)
    return summed_rows.reshape(blocks * size_block, channels) + own_rows.astype(F32)


def gathered_shards(
    features,
    tile_entries,
    tile_columns,
    tiles_per_row,
    rev_vals,
    rev_cols,
    rev_count,
    w_first,
    w_second,
    cotangent,
):
    channels = features.shape[1]
    pair = jnp.concatenate([features, cotangent], axis=1)
    pair_all = lax.all_gather(pair, AXES, axis=0, tiled=True)
    mixed_own = aggregate(
        tile_entries, tile_columns, tiles_per_row, pair_all[:, :channels], features
    ).astype(BF16)
    spread_own = aggregate(
        rev_vals, rev_cols, rev_count, pair_all[:, channels:], cotangent
    ).astype(BF16)
    both_all = lax.all_gather(
        jnp.concatenate([mixed_own, spread_own], axis=1), AXES, axis=0, tiled=True
    )
    mixed = both_all[:, :channels]
    spread = both_all[:, channels:]
    pre_first = jnp.dot(mixed, w_first, preferred_element_type=F32)
    sig = jax.nn.sigmoid(pre_first)
    hidden = (pre_first * sig).astype(BF16)
    slope = sig * (1.0 + pre_first * (1.0 - sig))
    back_hidden = lax.dot_general(
        spread, w_second, (((1,), (1,)), ((), ())), preferred_element_type=F32
    )
    back_first = (back_hidden * slope).astype(BF16)
    grad_first = lax.dot_general(
        mixed, back_first, (((0,), (0,)), ((), ())), preferred_element_type=F32
    )
    grad_second = lax.dot_general(
        hidden, spread, (((0,), (0,)), ((), ())), preferred_element_type=F32
    )
    position = lax.axis_index(AXES) * features.shape[0]
    hidden_own = lax.dynamic_slice_in_dim(hidden, position, features.shape[0], 0)
    mixed_second = aggregate(
        tile_entries, tile_columns, tiles_per_row, hidden, hidden_own
    ).astype(BF16)
    z_out = jnp.dot(mixed_second, w_second, preferred_element_type=F32).astype(BF16)
    return (z_out, grad_first, grad_second)


CORE, X, Y, XY = 1, 2, 4, 6
DEVICES, QUAD, PLANES, SLOTS, BLOCK = 32, 4, 4, 16, 64
LANES = 128
ROWS = 128
VMEM = pl.BlockSpec(memory_space=pltpu.VMEM)
SMEM = pl.BlockSpec(memory_space=pltpu.SMEM)
ANY = pl.BlockSpec(memory_space=pl.ANY)
PARAMS = pltpu.CompilerParams(vmem_limit_bytes=56 * 1024 * 1024)


def swap(value, mask):
    return lax.ppermute(value, AXES, [(i, i ^ mask) for i in range(DEVICES)])


def pack_body(pos, features, cotangent, codes, own, to_x, to_y, to_xy):
    for q, out in enumerate((own, to_x, to_y, to_xy)):
        first = pl.multiple_of((pos[0] ^ q) * LANES, LANES)
        out[:ROWS, :LANES] = features[:, pl.ds(first, LANES)]
        out[:ROWS, LANES:] = cotangent[:, pl.ds(first, LANES)]
        out[ROWS:, :] = codes[...]


def pack(pos, features, cotangent, codes):
    shape = jax.ShapeDtypeStruct((ROWS + 16, 2 * LANES), BF16)
    return pl.pallas_call(
        pack_body,
        out_shape=(shape,) * 4,
        in_specs=[SMEM, VMEM, VMEM, VMEM],
        out_specs=(VMEM,) * 4,
        compiler_params=PARAMS,
    )(pos, features, cotangent, codes)


def mix_body(codes, t0, t1, t2, t3, t4, a0, a1, a2, a3, out, table, picked, sems):
    span = QUAD * ROWS
    copies = []
    for i, (ref, size) in enumerate(((t0, 1), (t1, 1), (t2, 1), (t3, 1), (t4, 4))):
        copies.append(
            pltpu.make_async_copy(ref, table.at[pl.ds(i * span, size * span), :], sems.at[i])
        )
        copies[-1].start()
    table[DEVICES * ROWS :, :] = jnp.zeros((BLOCK, LANES), BF16)
    for copy in copies:
        copy.wait()
    for q, tiles in enumerate((a0, a1, a2, a3)):
        for w in range(2):
            row = q * 2 + w
            for s in range(SLOTS):
                first = pl.multiple_of(codes[row * SLOTS + s] * BLOCK, BLOCK)
                picked[row, pl.ds(s * BLOCK, BLOCK), :] = table[pl.ds(first, BLOCK), :]
            total = jnp.dot(tiles[w], picked[row], preferred_element_type=F32)
            total = total + table[pl.ds(row * BLOCK, BLOCK), :].astype(F32)
            out[pl.ds(row * BLOCK, BLOCK), :] = total.astype(BF16)


def mix(codes, planes, other_core, tiles):
    return pl.pallas_call(
        mix_body,
        out_shape=jax.ShapeDtypeStruct((QUAD * ROWS, LANES), BF16),
        in_specs=[SMEM] + [ANY] * 5 + [VMEM] * 4,
        out_specs=VMEM,
        scratch_shapes=[
            pltpu.VMEM((DEVICES * ROWS + BLOCK, LANES), BF16),
            pltpu.VMEM((2 * QUAD, SLOTS * BLOCK, LANES), BF16),
            pltpu.SemaphoreType.DMA((5,)),
        ],
        compiler_params=PARAMS,
    )(codes, *planes, other_core, *tiles)


def assemble(pos, pieces, target, sems):
    copies = []
    for j in range(PLANES):
        for p in range(QUAD):
            column = pos[0] ^ p
            for q in range(QUAD):
                row = ((pos[1] ^ j) * QUAD + (column ^ q)) * ROWS
                copies.append(
                    pltpu.make_async_copy(
                        pieces[j * QUAD + p].at[pl.ds(q * ROWS, ROWS), :],
                        target.at[
                            pl.ds(pl.multiple_of(row, ROWS), ROWS),
                            pl.ds(pl.multiple_of(column * LANES, LANES), LANES),
                        ],
                        sems.at[len(copies)],
                    )
                )
                copies[-1].start()
    for copy in copies:
        copy.wait()


def first_body(pos, *refs):
    pieces = refs[:16]
    w_first, mixed, hidden, slope, sems = refs[16:]
    assemble(pos, pieces, mixed, sems)
    chunk = QUAD * ROWS
    for z in range(PLANES):
        rows = pl.ds(z * chunk, chunk)
        pre = jnp.dot(mixed[rows, :], w_first[...], preferred_element_type=F32)
        sig = jax.nn.sigmoid(pre)
        hidden[rows, :] = (pre * sig).astype(BF16)
        slope[rows, :] = sig * (1.0 + pre * (1.0 - sig))


def first_layer(pos, pieces, w_first):
    count, channels = PLANES * QUAD * ROWS, w_first.shape[0]
    return pl.pallas_call(
        first_body,
        out_shape=(
            jax.ShapeDtypeStruct((count, channels), BF16),
            jax.ShapeDtypeStruct((count, channels), BF16),
            jax.ShapeDtypeStruct((count, channels), F32),
        ),
        in_specs=[SMEM] + [ANY] * 16 + [VMEM],
        out_specs=(VMEM,) * 3,
        scratch_shapes=[pltpu.SemaphoreType.DMA((64,))],
        compiler_params=PARAMS,
    )(pos, *pieces, w_first)


def second_body(codes, mine, other, tiles, w_second, z_out, picked, own, sems):
    count = 2 * SLOTS

    def fetch(slot, source, row):
        return pltpu.make_async_copy(
            source.at[pl.ds(pl.multiple_of(row, BLOCK), BLOCK), :],
            picked.at[pl.ds(slot * BLOCK, BLOCK), :],
            sems.at[slot],
        )

    own_copy = pltpu.make_async_copy(
        mine.at[pl.ds(pl.multiple_of(codes[2 * count], ROWS), ROWS), :], own, sems.at[count]
    )
    own_copy.start()
    for slot in range(count):
        kind, row = codes[slot], codes[count + slot]

        @pl.when(kind == 0)
        def _():
            fetch(slot, mine, row).start()

        @pl.when(kind == 1)
        def _():
            fetch(slot, other, row).start()

        @pl.when(kind == 2)
        def _():
            picked[pl.ds(slot * BLOCK, BLOCK), :] = jnp.zeros((BLOCK, picked.shape[1]), BF16)

    own_copy.wait()
    for w in range(2):
        for s in range(SLOTS):
            slot = w * SLOTS + s

            @pl.when(codes[slot] != 2)
            def _():
                fetch(slot, mine, 0).wait()

        total = jnp.dot(
            tiles[w],
            picked[pl.ds(w * SLOTS * BLOCK, SLOTS * BLOCK), :],
            preferred_element_type=F32,
        )
        total = total + own[pl.ds(w * BLOCK, BLOCK), :].astype(F32)
        own[pl.ds(w * BLOCK, BLOCK), :] = total.astype(BF16)
    z_out[...] = jnp.dot(own[...], w_second[...], preferred_element_type=F32).astype(BF16)


def second_layer(codes, mine, other, tiles, w_second):
    channels = w_second.shape[0]
    return pl.pallas_call(
        second_body,
        out_shape=jax.ShapeDtypeStruct((ROWS, channels), BF16),
        in_specs=[SMEM, ANY, ANY, VMEM, VMEM],
        out_specs=VMEM,
        scratch_shapes=[
            pltpu.VMEM((2 * SLOTS * BLOCK, channels), BF16),
            pltpu.VMEM((ROWS, channels), BF16),
            pltpu.SemaphoreType.DMA((2 * SLOTS + 1,)),
        ],
        compiler_params=PARAMS,
    )(codes, mine, other, tiles, w_second)


def grads_body(pos, *refs):
    pieces = refs[:16]
    mixed, hidden, slope, w_second, out, spread, sems = refs[16:]
    assemble(pos, pieces, spread, sems)
    channels = w_second.shape[0]
    chunk = QUAD * ROWS
    for z in range(PLANES):
        rows = pl.ds(z * chunk, chunk)
        back_hidden = lax.dot_general(
            spread[rows, :], w_second[...], (((1,), (1,)), ((), ())), preferred_element_type=F32
        )
        back_first = (back_hidden * slope[rows, :]).astype(BF16)
        part_first = lax.dot_general(
            mixed[rows, :], back_first, (((0,), (0,)), ((), ())), preferred_element_type=F32
        )
        part_second = lax.dot_general(
            hidden[rows, :], spread[rows, :], (((0,), (0,)), ((), ())), preferred_element_type=F32
        )
        if z == 0:
            out[:channels, :] = part_first
            out[channels:, :] = part_second
        else:
            out[:channels, :] += part_first
            out[channels:, :] += part_second


def gradients(pos, pieces, mixed, hidden, slope, w_second):
    channels = w_second.shape[0]
    return pl.pallas_call(
        grads_body,
        out_shape=jax.ShapeDtypeStruct((2 * channels, channels), F32),
        in_specs=[SMEM] + [ANY] * 16 + [VMEM] * 4,
        out_specs=VMEM,
        scratch_shapes=[
            pltpu.VMEM((PLANES * QUAD * ROWS, channels), BF16),
            pltpu.SemaphoreType.DMA((64,)),
        ],
        compiler_params=PARAMS,
    )(pos, *pieces, mixed, hidden, slope, w_second)


def class_gather(piece, early, late):
    pieces = []
    for j in range(PLANES):
        here = piece if j == 0 else swap(piece, 8 * j)
        by_early = swap(here, early)
        by_late = swap(here, late)
        by_both = swap(by_early, late)
        by_x, by_y = (by_early, by_late) if early == X else (by_late, by_early)
        pieces += [here, by_x, by_y, by_both]
    return pieces


def planned_shards(
    features,
    tile_entries,
    tile_columns,
    tiles_per_row,
    rev_vals,
    rev_cols,
    rev_count,
    w_first,
    w_second,
    cotangent,
):
    device = lax.axis_index(AXES)
    pos = jnp.stack([(device >> 1) & 3, device >> 3]).astype(jnp.int32)
    columns = jnp.concatenate([tile_columns, rev_cols], axis=0)
    counts = jnp.concatenate([tiles_per_row, rev_count], axis=0)
    slot_ids = lax.broadcasted_iota(jnp.int32, columns.shape, 1)
    codes = jnp.where(slot_ids < counts[:, None], columns, -1)
    codes_padded = jnp.pad(codes.astype(BF16), ((0, 12), (0, 2 * LANES - SLOTS)))
    packed = pack(pos, features, cotangent, codes_padded)
    parts = [packed[0]] + [swap(packed[q], 2 * q) for q in range(1, 4)]

    near = jnp.stack([part[ROWS : ROWS + 4, :SLOTS] for part in parts]).astype(jnp.int32)
    apart = (near >> 1) ^ device
    address = ((apart & 1) * 16 + (apart >> 3) * 4 + ((apart >> 1) & 3)) * 2 + (near & 1)
    address = jnp.where(near < 0, 2 * DEVICES, address)

    def slices(first):
        return jnp.concatenate([part[:ROWS, first : first + LANES] for part in parts], axis=0)

    def phase(first, tiles_own, rows):
        piece = slices(first)
        planes = [piece] + [swap(piece, 8 * j) for j in range(1, 4)]
        other_core = swap(jnp.concatenate(planes, axis=0), CORE)
        tiles = [tiles_own] + [swap(tiles_own, 2 * q) for q in range(1, 4)]
        return mix(address[:, rows : rows + 2].reshape(-1), planes, other_core, tiles)

    mixed_piece = phase(0, tile_entries, 0)
    spread_piece = phase(LANES, rev_vals, 2)
    mixed, hidden, slope = first_layer(pos, class_gather(mixed_piece, X, Y), w_first)
    hidden_other = swap(hidden, CORE)
    live = codes[:2]
    kind = jnp.where(live < 0, 2, ((live >> 1) ^ device) & 1).reshape(-1)
    row = ((live >> 2) * ROWS + (live & 1) * BLOCK).reshape(-1)
    second_codes = jnp.concatenate([kind, row, ((device >> 1) * ROWS)[None]]).astype(jnp.int32)
    z_out = second_layer(second_codes, hidden, hidden_other, tile_entries, w_second)
    part = gradients(pos, class_gather(spread_piece, Y, X), mixed, hidden, slope, w_second)
    total = part + swap(part, CORE)
    channels = w_second.shape[0]
    return (z_out, total[:channels], total[channels:])


def solution(mesh):
    placed = (
        P(AXES, None),
        P(AXES, None, None),
        P(AXES, None),
        P(AXES),
        P(AXES, None, None),
        P(AXES, None),
        P(AXES),
        P(),
        P(),
        P(AXES, None),
    )
    planned = mesh.shape["rows"] == 8 and mesh.shape["grp"] == 4
    return jax.shard_map(
        planned_shards if planned else gathered_shards,
        mesh=mesh,
        in_specs=placed,
        out_specs=(P(AXES, None), P(), P()),
        check_vma=False,
    )
```

```python
import functools

import jax
import jax.numpy as jnp
from jax import lax
from jax.experimental import pallas as pl
from jax.experimental.pallas import tpu as pltpu
from jax.sharding import PartitionSpec as P

AXES = ("rows", "grp")
F32 = jnp.float32
BF16 = jnp.bfloat16


def aggregate(panel_vals, strip_columns, strip_count, everyone, own_rows):
    blocks, size_block, span_width = panel_vals.shape
    slot_count = span_width // size_block
    channels = everyone.shape[1]
    block_table = everyone.reshape(-1, size_block, channels)
    slot_ids = lax.broadcasted_iota(jnp.int32, strip_columns.shape, 1)
    weights = (slot_ids < strip_count[:, None]).astype(everyone.dtype)
    picked = (block_table[strip_columns] * weights[:, :, None, None]).reshape(
        blocks, slot_count * size_block, channels
    )
    summed_rows = jnp.einsum("bik,bkc->bic", panel_vals, picked, preferred_element_type=F32)
    return summed_rows.reshape(blocks * size_block, channels) + own_rows.astype(F32)


def gathered_shards(
    features,
    tile_entries,
    tile_columns,
    tiles_per_row,
    rev_vals,
    rev_cols,
    rev_count,
    w_first,
    w_second,
    cotangent,
):
    channels = features.shape[1]
    pair = jnp.concatenate([features, cotangent], axis=1)
    pair_all = lax.all_gather(pair, AXES, axis=0, tiled=True)
    mixed_own = aggregate(
        tile_entries, tile_columns, tiles_per_row, pair_all[:, :channels], features
    ).astype(BF16)
    spread_own = aggregate(
        rev_vals, rev_cols, rev_count, pair_all[:, channels:], cotangent
    ).astype(BF16)
    both_all = lax.all_gather(
        jnp.concatenate([mixed_own, spread_own], axis=1), AXES, axis=0, tiled=True
    )
    mixed = both_all[:, :channels]
    spread = both_all[:, channels:]
    pre_first = jnp.dot(mixed, w_first, preferred_element_type=F32)
    sig = jax.nn.sigmoid(pre_first)
    hidden = (pre_first * sig).astype(BF16)
    slope = sig * (1.0 + pre_first * (1.0 - sig))
    back_hidden = lax.dot_general(
        spread, w_second, (((1,), (1,)), ((), ())), preferred_element_type=F32
    )
    back_first = (back_hidden * slope).astype(BF16)
    grad_first = lax.dot_general(
        mixed, back_first, (((0,), (0,)), ((), ())), preferred_element_type=F32
    )
    grad_second = lax.dot_general(
        hidden, spread, (((0,), (0,)), ((), ())), preferred_element_type=F32
    )
    position = lax.axis_index(AXES) * features.shape[0]
    hidden_own = lax.dynamic_slice_in_dim(hidden, position, features.shape[0], 0)
    mixed_second = aggregate(
        tile_entries, tile_columns, tiles_per_row, hidden, hidden_own
    ).astype(BF16)
    z_out = jnp.dot(mixed_second, w_second, preferred_element_type=F32).astype(BF16)
    return (z_out, grad_first, grad_second)


CORE = 1
DEVICES, QUAD, PLANES, SLOTS, BLOCK = 32, 4, 4, 16, 64
LANES = 128
ROWS = 128
SPAN = QUAD * ROWS
VMEM = pl.BlockSpec(memory_space=pltpu.VMEM)
SMEM = pl.BlockSpec(memory_space=pltpu.SMEM)
ANY = pl.BlockSpec(memory_space=pl.ANY)
PARAMS = pltpu.CompilerParams(vmem_limit_bytes=48 * 1024 * 1024)


def call(body, out_shape, operands, spaces, scratch=()):
    return pl.pallas_call(
        body,
        out_shape=out_shape,
        in_specs=list(spaces),
        out_specs=jax.tree.map(lambda _: VMEM, out_shape),
        scratch_shapes=list(scratch),
        compiler_params=PARAMS,
    )(*operands)


def shaped(rows, columns, dtype=BF16):
    return jax.ShapeDtypeStruct((rows, columns), dtype)


def swap(value, mask):
    return lax.ppermute(value, AXES, [(i, i ^ mask) for i in range(DEVICES)])


def over_quad(value):
    return [value] + [swap(value, 2 * q) for q in range(1, QUAD)]


def over_planes(value):
    return [value] + [swap(value, 8 * j) for j in range(1, PLANES)]


def chip(pos):
    return (pos[0] >> 1) & 3


def lanes_of(column):
    return pl.ds(pl.multiple_of(column * LANES, LANES), LANES)


def pack_body(pos, columns, counts, back_columns, back_counts, features, cotangent, *outs):
    line = lax.broadcasted_iota(jnp.int32, (16, LANES), 0)
    lane = lax.broadcasted_iota(jnp.int32, (16, LANES), 1)
    codes = jnp.full((16, LANES), -1, jnp.int32)
    for r, (table, count) in enumerate(((columns, counts), (back_columns, back_counts))):
        for w in range(2):
            for s in range(SLOTS):
                value = jnp.where(s < count[w], table[w, s], -1)
                codes = jnp.where((line == 2 * r + w) & (lane == s), value, codes)
    codes = codes.astype(F32).astype(BF16)
    for q, out in enumerate(outs):
        share = lanes_of(chip(pos) ^ q)
        out[:ROWS, :LANES] = features[:, share]
        out[:ROWS, LANES:] = cotangent[:, share]
        out[ROWS:, :LANES] = codes
        out[ROWS:, LANES:] = codes


def pack(pos, columns, counts, back_columns, back_counts, features, cotangent):
    return call(
        pack_body,
        (shaped(ROWS + 16, 2 * LANES),) * QUAD,
        (pos, columns, counts, back_columns, back_counts, features, cotangent),
        [SMEM] * 5 + [VMEM] * 2,
    )


def unpack_body(pos, *refs):
    parts, (forward, backward, places) = refs[:QUAD], refs[QUAD:]
    for q, part in enumerate(parts):
        rows = pl.ds(q * ROWS, ROWS)
        forward[rows, :] = part[:ROWS, :LANES]
        backward[rows, :] = part[:ROWS, LANES:]
        block = part[ROWS:, :LANES].astype(F32).astype(jnp.int32)
        apart = (block >> 1) ^ pos[0]
        place = ((apart & 1) * 16 + (apart >> 3) * 4 + ((apart >> 1) & 3)) * 2 + (block & 1)
        place = jnp.where(block < 0, 2 * DEVICES, place)
        places[q * 8 : q * 8 + 8, :] = place[:8, :]


def unpack(pos, parts):
    return call(
        unpack_body,
        (shaped(SPAN, LANES), shaped(SPAN, LANES), shaped(8 * QUAD, LANES, jnp.int32)),
        (pos, *parts),
        [SMEM] + [VMEM] * QUAD,
    )


def mix_body(base, split, places, *refs):
    shares, tiles, outs = refs[:8], refs[8:12], refs[12:-3]
    table, picked, sems = refs[-3:]
    copies = []
    for i, share in enumerate(shares):
        copies.append(pltpu.make_async_copy(share, table.at[pl.ds(i * SPAN, SPAN), :], sems.at[i]))
        copies[-1].start()
    table[DEVICES * ROWS :, :] = jnp.zeros((BLOCK, LANES), BF16)
    for copy in copies:
        copy.wait()
    for q in range(QUAD):
        for w in range(2):
            row = q * 2 + w
            for s in range(SLOTS):
                first = pl.multiple_of(places[q * 8 + base + w, s] * BLOCK, BLOCK)
                picked[row, pl.ds(s * BLOCK, BLOCK), :] = table[pl.ds(first, BLOCK), :]
            total = jnp.dot(tiles[q][w], picked[row], preferred_element_type=F32)
            total = total + table[pl.ds(row * BLOCK, BLOCK), :].astype(F32)
            if split:
                outs[q][pl.ds(w * BLOCK, BLOCK), :] = total.astype(BF16)
            else:
                outs[0][pl.ds(row * BLOCK, BLOCK), :] = total.astype(BF16)


def mix(places, base, planes, other_core, tiles, split=False):
    return call(
        functools.partial(mix_body, base, split),
        (shaped(ROWS, LANES),) * QUAD if split else (shaped(SPAN, LANES),),
        (places, *planes, *other_core, *tiles),
        [SMEM] + [ANY] * 8 + [VMEM] * 4,
        [
            pltpu.VMEM((DEVICES * ROWS + BLOCK, LANES), BF16),
            pltpu.VMEM((2 * QUAD, SLOTS * BLOCK, LANES), BF16),
            pltpu.SemaphoreType.DMA((8,)),
        ],
    )


def whole_rows(pos, pieces, target):
    for p, piece in enumerate(pieces):
        share = lanes_of(chip(pos) ^ p)
        for q in range(QUAD):
            target[pl.ds(q * ROWS, ROWS), share] = piece[pl.ds((p ^ q) * ROWS, ROWS), :]


def first_body(pos, p0, p1, p2, p3, w_first, mixed, hidden, hidden_share, slope, full):
    whole_rows(pos, (p0, p1, p2, p3), mixed)
    pre = jnp.dot(mixed[...], w_first[...], preferred_element_type=F32)
    sig = jax.nn.sigmoid(pre)
    hidden[...] = (pre * sig).astype(BF16)
    full[...] = sig * (1.0 + pre * (1.0 - sig))
    share = lanes_of(chip(pos))
    hidden_share[...] = hidden[:, share]
    slope[...] = full[:, share]


def first_layer(pos, pieces, w_first):
    channels = w_first.shape[0]
    return call(
        first_body,
        (
            shaped(SPAN, channels),
            shaped(SPAN, channels),
            shaped(SPAN, LANES),
            shaped(SPAN, LANES, F32),
        ),
        (pos, *pieces, w_first),
        [SMEM] + [VMEM] * 5,
        [pltpu.VMEM((SPAN, channels), F32)],
    )


def second_body(pos, p0, p1, p2, p3, w_second, z_out):
    total = jnp.zeros(z_out.shape, F32)
    for p, piece in enumerate((p0, p1, p2, p3)):
        total = total + jnp.dot(
            piece[...], w_second[lanes_of(chip(pos) ^ p), :], preferred_element_type=F32
        )
    z_out[...] = total.astype(BF16)


def second_layer(pos, pieces, w_second):
    return call(
        second_body,
        shaped(ROWS, w_second.shape[0]),
        (pos, *pieces, w_second),
        [SMEM] + [VMEM] * 5,
    )


def grads_body(pos, mixed, hidden, slope, p0, p1, p2, p3, w_second, keep, send, spread):
    whole_rows(pos, (p0, p1, p2, p3), spread)
    back_hidden = lax.dot_general(
        spread[...],
        w_second[lanes_of(chip(pos)), :],
        (((1,), (1,)), ((), ())),
        preferred_element_type=F32,
    )
    back_first = (back_hidden * slope[...]).astype(BF16)
    over_rows = (((0,), (0,)), ((), ()))
    first = lax.dot_general(mixed[...], back_first, over_rows, preferred_element_type=F32)
    second = lax.dot_general(hidden[...], p0[...], over_rows, preferred_element_type=F32)
    keeps_first = (pos[0] & 1) == 0

    @pl.when(keeps_first)
    def _():
        keep[...] = first
        send[...] = second

    @pl.when(jnp.logical_not(keeps_first))
    def _():
        keep[...] = second
        send[...] = first


def gradients(pos, mixed, hidden, slope, pieces, w_second):
    channels = w_second.shape[0]
    return call(
        grads_body,
        (shaped(channels, LANES, F32), shaped(channels, LANES, F32)),
        (pos, mixed, hidden, slope, *pieces, w_second),
        [SMEM] + [VMEM] * 8,
        [pltpu.VMEM((SPAN, channels), BF16)],
    )


def place_body(pos, *refs):
    mine, other, (first, second) = refs[:QUAD], refs[QUAD : 2 * QUAD], refs[2 * QUAD :]
    keeps_first = (pos[0] & 1) == 0

    def fill(mine_out, other_out):
        for p in range(QUAD):
            share = lanes_of(chip(pos) ^ p)
            mine_out[:, share] = mine[p][...].astype(F32)
            other_out[:, share] = other[p][...].astype(F32)

    @pl.when(keeps_first)
    def _():
        fill(first, second)

    @pl.when(jnp.logical_not(keeps_first))
    def _():
        fill(second, first)


def place(pos, mine, other):
    channels = mine[0].shape[0]
    return call(
        place_body,
        (shaped(channels, channels, F32),) * 2,
        (pos, *mine, *other),
        [SMEM] + [VMEM] * (2 * QUAD),
    )


def planned_shards(
    features,
    tile_entries,
    tile_columns,
    tiles_per_row,
    rev_vals,
    rev_cols,
    rev_count,
    w_first,
    w_second,
    cotangent,
):
    pos = lax.axis_index(AXES).astype(jnp.int32).reshape(1)
    packed = pack(pos, tile_columns, tiles_per_row, rev_cols, rev_count, features, cotangent)
    parts = [packed[0]] + [swap(packed[q], 2 * q) for q in range(1, QUAD)]
    forward, backward, places = unpack(pos, parts)
    tile_entries, _ = lax.optimization_barrier((tile_entries, parts[1]))
    tiles = over_quad(tile_entries)
    rev_vals, _ = lax.optimization_barrier((rev_vals, tiles[1]))
    back_tiles = over_quad(rev_vals)

    def both_cores(share):
        planes = over_planes(share)
        return planes, [swap(plane, CORE) for plane in planes]

    (mixed_share,) = mix(places, 0, *both_cores(forward), tiles)
    (spread_share,) = mix(places, 2, *both_cores(backward), back_tiles)
    mixed, hidden, hidden_share, slope = first_layer(pos, over_quad(mixed_share), w_first)
    again = mix(places, 0, *both_cores(hidden_share), tiles, split=True)
    z_out = second_layer(
        pos, [again[0]] + [swap(again[q], 2 * q) for q in range(1, QUAD)], w_second
    )
    keep, send = gradients(pos, mixed, hidden, slope, over_quad(spread_share), w_second)
    part = (keep + swap(send, CORE)).astype(BF16)
    near, z1, z2, z3 = (plane.astype(F32) for plane in over_planes(part))
    total = ((near + z1) + (z2 + z3)).astype(BF16)
    mine = over_quad(total)
    grad_first, grad_second = place(pos, mine, [swap(piece, CORE) for piece in mine])
    return (z_out, grad_first, grad_second)


def solution(mesh):
    placed = (
        P(AXES, None),
        P(AXES, None, None),
        P(AXES, None),
        P(AXES),
        P(AXES, None, None),
        P(AXES, None),
        P(AXES),
        P(),
        P(),
        P(AXES, None),
    )
    planned = mesh.shape["rows"] == 8 and mesh.shape["grp"] == 4
    return jax.shard_map(
        planned_shards if planned else gathered_shards,
        mesh=mesh,
        in_specs=placed,
        out_specs=(P(AXES, None), P(), P()),
        check_vma=False,
    )
```

```python
import functools

import jax
import jax.numpy as jnp
from jax import lax
from jax.experimental import pallas as pl
from jax.experimental.pallas import tpu as pltpu
from jax.sharding import PartitionSpec as P

AXES = ("rows", "grp")
F32 = jnp.float32
BF16 = jnp.bfloat16


def aggregate(panel_vals, strip_columns, strip_count, everyone, own_rows):
    blocks, size_block, span_width = panel_vals.shape
    slot_count = span_width // size_block
    channels = everyone.shape[1]
    block_table = everyone.reshape(-1, size_block, channels)
    slot_ids = lax.broadcasted_iota(jnp.int32, strip_columns.shape, 1)
    weights = (slot_ids < strip_count[:, None]).astype(everyone.dtype)
    picked = (block_table[strip_columns] * weights[:, :, None, None]).reshape(
        blocks, slot_count * size_block, channels
    )
    summed_rows = jnp.einsum("bik,bkc->bic", panel_vals, picked, preferred_element_type=F32)
    return summed_rows.reshape(blocks * size_block, channels) + own_rows.astype(F32)


def gathered_shards(
    features,
    tile_entries,
    tile_columns,
    tiles_per_row,
    rev_vals,
    rev_cols,
    rev_count,
    w_first,
    w_second,
    cotangent,
):
    channels = features.shape[1]
    pair = jnp.concatenate([features, cotangent], axis=1)
    pair_all = lax.all_gather(pair, AXES, axis=0, tiled=True)
    mixed_own = aggregate(
        tile_entries, tile_columns, tiles_per_row, pair_all[:, :channels], features
    ).astype(BF16)
    spread_own = aggregate(
        rev_vals, rev_cols, rev_count, pair_all[:, channels:], cotangent
    ).astype(BF16)
    both_all = lax.all_gather(
        jnp.concatenate([mixed_own, spread_own], axis=1), AXES, axis=0, tiled=True
    )
    mixed = both_all[:, :channels]
    spread = both_all[:, channels:]
    pre_first = jnp.dot(mixed, w_first, preferred_element_type=F32)
    sig = jax.nn.sigmoid(pre_first)
    hidden = (pre_first * sig).astype(BF16)
    slope = sig * (1.0 + pre_first * (1.0 - sig))
    back_hidden = lax.dot_general(
        spread, w_second, (((1,), (1,)), ((), ())), preferred_element_type=F32
    )
    back_first = (back_hidden * slope).astype(BF16)
    grad_first = lax.dot_general(
        mixed, back_first, (((0,), (0,)), ((), ())), preferred_element_type=F32
    )
    grad_second = lax.dot_general(
        hidden, spread, (((0,), (0,)), ((), ())), preferred_element_type=F32
    )
    position = lax.axis_index(AXES) * features.shape[0]
    hidden_own = lax.dynamic_slice_in_dim(hidden, position, features.shape[0], 0)
    mixed_second = aggregate(
        tile_entries, tile_columns, tiles_per_row, hidden, hidden_own
    ).astype(BF16)
    z_out = jnp.dot(mixed_second, w_second, preferred_element_type=F32).astype(BF16)
    return (z_out, grad_first, grad_second)


CORE = 1
DEVICES, QUAD, PLANES, SLOTS, BLOCK = 32, 4, 4, 16, 64
LANES = 128
ROWS = 128
SPAN = QUAD * ROWS
VMEM = pl.BlockSpec(memory_space=pltpu.VMEM)
SMEM = pl.BlockSpec(memory_space=pltpu.SMEM)
ANY = pl.BlockSpec(memory_space=pl.ANY)
PARAMS = pltpu.CompilerParams(vmem_limit_bytes=48 * 1024 * 1024)


def call(body, out_shape, operands, spaces, scratch=()):
    return pl.pallas_call(
        body,
        out_shape=out_shape,
        in_specs=list(spaces),
        out_specs=jax.tree.map(lambda _: VMEM, out_shape),
        scratch_shapes=list(scratch),
        compiler_params=PARAMS,
    )(*operands)


def shaped(rows, columns, dtype=BF16):
    return jax.ShapeDtypeStruct((rows, columns), dtype)


def swap(value, mask):
    return lax.ppermute(value, AXES, [(i, i ^ mask) for i in range(DEVICES)])


def over_quad(value):
    return [value] + [swap(value, 2 * q) for q in range(1, QUAD)]


def over_planes(value):
    second = swap(value, 16)
    return [value, swap(value, 8), second, swap(second, 8)]


def chip(pos):
    return (pos[0] >> 1) & 3


def lanes_of(column):
    return pl.ds(pl.multiple_of(column * LANES, LANES), LANES)


def pack_body(pos, *refs):
    tables, (features, cotangent, tiles, back_tiles) = refs[:4], refs[4:8]
    outs, both_tiles, scalars, sems = refs[8:12], refs[12], refs[13:17], refs[17]
    copies = [(table, scalar) for table, scalar in zip(tables, scalars)]
    for q, out in enumerate(outs):
        share = lanes_of(chip(pos) ^ q)
        copies.append((features.at[:, share], out.at[pl.ds(0, ROWS), pl.ds(0, LANES)]))
        copies.append((cotangent.at[:, share], out.at[pl.ds(0, ROWS), pl.ds(LANES, LANES)]))
    copies.append((tiles, both_tiles.at[pl.ds(0, 2)]))
    copies.append((back_tiles, both_tiles.at[pl.ds(2, 2)]))
    copies = [pltpu.make_async_copy(a, b, sems.at[i]) for i, (a, b) in enumerate(copies)]
    for copy in copies:
        copy.start()
    for copy in copies[:4]:
        copy.wait()
    line = lax.broadcasted_iota(jnp.int32, (16, LANES), 0)
    lane = lax.broadcasted_iota(jnp.int32, (16, LANES), 1)
    codes = jnp.full((16, LANES), -1, jnp.int32)
    for r in range(2):
        table, count = scalars[2 * r], scalars[2 * r + 1]
        for w in range(2):
            for s in range(SLOTS):
                value = jnp.where(s < count[w], table[w, s], -1)
                codes = jnp.where((line == 2 * r + w) & (lane == s), value, codes)
    codes = codes.astype(F32).astype(BF16)
    for out in outs:
        out[ROWS:, :LANES] = codes
        out[ROWS:, LANES:] = codes
    for copy in copies[4:]:
        copy.wait()


def pack(pos, columns, counts, back_columns, back_counts, features, cotangent, tiles, back_tiles):
    return call(
        pack_body,
        (shaped(ROWS + 16, 2 * LANES),) * QUAD
        + (jax.ShapeDtypeStruct((4, BLOCK, SLOTS * BLOCK), BF16),),
        (pos, columns, counts, back_columns, back_counts, features, cotangent, tiles, back_tiles),
        [SMEM] + [ANY] * 8,
        [pltpu.SMEM((2, SLOTS), jnp.int32), pltpu.SMEM((2,), jnp.int32)] * 2
        + [pltpu.SemaphoreType.DMA((14,))],
    )


def unpack_body(pos, *refs):
    parts, (both, places) = refs[:QUAD], refs[QUAD:]
    for q, part in enumerate(parts):
        both[pl.ds(q * ROWS, ROWS), :] = part[:ROWS, :]
        block = part[ROWS:, :LANES].astype(F32).astype(jnp.int32)
        apart = (block >> 1) ^ pos[0]
        place = ((apart & 1) * 16 + (apart >> 3) * 4 + ((apart >> 1) & 3)) * 2 + (block & 1)
        place = jnp.where(block < 0, 2 * DEVICES, place)
        places[q * 8 : q * 8 + 8, :] = place[:8, :]


def unpack(pos, parts):
    return call(
        unpack_body,
        (shaped(SPAN, 2 * LANES), shaped(8 * QUAD, LANES, jnp.int32)),
        (pos, *parts),
        [SMEM] + [VMEM] * QUAD,
    )


def mix_body(base, half, split, places, *refs):
    shares, tiles, outs = refs[:8], refs[8:12], refs[12:-3]
    table, picked, sems = refs[-3:]
    copies = []
    for i, share in enumerate(shares):
        copies.append(
            pltpu.make_async_copy(
                share.at[:, pl.ds(half * LANES, LANES)],
                table.at[pl.ds(i * SPAN, SPAN), :],
                sems.at[i],
            )
        )
        copies[-1].start()
    table[DEVICES * ROWS :, :] = jnp.zeros((BLOCK, LANES), BF16)
    for copy in copies:
        copy.wait()
    for q in range(QUAD):
        for w in range(2):
            row = q * 2 + w
            for s in range(SLOTS):
                first = pl.multiple_of(places[q * 8 + base + w, s] * BLOCK, BLOCK)
                picked[row, pl.ds(s * BLOCK, BLOCK), :] = table[pl.ds(first, BLOCK), :]
            total = jnp.dot(tiles[q][base + w], picked[row], preferred_element_type=F32)
            total = total + table[pl.ds(row * BLOCK, BLOCK), :].astype(F32)
            if split:
                outs[q][pl.ds(w * BLOCK, BLOCK), :] = total.astype(BF16)
            else:
                outs[0][pl.ds(row * BLOCK, BLOCK), :] = total.astype(BF16)


def mix(places, base, half, shares, tiles, split=False):
    return call(
        functools.partial(mix_body, base, half, split),
        (shaped(ROWS, LANES),) * QUAD if split else (shaped(SPAN, LANES),),
        (places, *shares, *tiles),
        [SMEM] + [ANY] * 8 + [VMEM] * 4,
        [
            pltpu.VMEM((DEVICES * ROWS + BLOCK, LANES), BF16),
            pltpu.VMEM((2 * QUAD, SLOTS * BLOCK, LANES), BF16),
            pltpu.SemaphoreType.DMA((8,)),
        ],
    )


def whole_rows(pos, pieces, target):
    for p, piece in enumerate(pieces):
        share = lanes_of(chip(pos) ^ p)
        for q in range(QUAD):
            target[pl.ds(q * ROWS, ROWS), share] = piece[pl.ds((p ^ q) * ROWS, ROWS), :]


def first_body(pos, p0, p1, p2, p3, w_first, mixed, hidden, hidden_share, slope, full):
    whole_rows(pos, (p0, p1, p2, p3), mixed)
    pre = jnp.dot(mixed[...], w_first[...], preferred_element_type=F32)
    sig = jax.nn.sigmoid(pre)
    hidden[...] = (pre * sig).astype(BF16)
    full[...] = sig * (1.0 + pre * (1.0 - sig))
    share = lanes_of(chip(pos))
    hidden_share[...] = hidden[:, share]
    slope[...] = full[:, share]


def first_layer(pos, pieces, w_first):
    channels = w_first.shape[0]
    return call(
        first_body,
        (
            shaped(SPAN, channels),
            shaped(SPAN, channels),
            shaped(SPAN, LANES),
            shaped(SPAN, LANES, F32),
        ),
        (pos, *pieces, w_first),
        [SMEM] + [VMEM] * 5,
        [pltpu.VMEM((SPAN, channels), F32)],
    )


def second_body(pos, p0, p1, p2, p3, w_second, z_out):
    total = jnp.zeros(z_out.shape, F32)
    for p, piece in enumerate((p0, p1, p2, p3)):
        total = total + jnp.dot(
            piece[...], w_second[lanes_of(chip(pos) ^ p), :], preferred_element_type=F32
        )
    z_out[...] = total.astype(BF16)


def second_layer(pos, pieces, w_second):
    return call(
        second_body,
        shaped(ROWS, w_second.shape[0]),
        (pos, *pieces, w_second),
        [SMEM] + [VMEM] * 5,
    )


def grads_body(pos, mixed, hidden, slope, p0, p1, p2, p3, w_second, keep, send, spread):
    whole_rows(pos, (p0, p1, p2, p3), spread)
    back_hidden = lax.dot_general(
        spread[...],
        w_second[lanes_of(chip(pos)), :],
        (((1,), (1,)), ((), ())),
        preferred_element_type=F32,
    )
    back_first = (back_hidden * slope[...]).astype(BF16)
    over_rows = (((0,), (0,)), ((), ()))
    first = lax.dot_general(mixed[...], back_first, over_rows, preferred_element_type=F32)
    second = lax.dot_general(hidden[...], p0[...], over_rows, preferred_element_type=F32)
    keeps_first = (pos[0] & 1) == 0

    @pl.when(keeps_first)
    def _():
        keep[...] = first
        send[...] = second

    @pl.when(jnp.logical_not(keeps_first))
    def _():
        keep[...] = second
        send[...] = first


def gradients(pos, mixed, hidden, slope, pieces, w_second):
    channels = w_second.shape[0]
    return call(
        grads_body,
        (shaped(channels, LANES, F32), shaped(channels, LANES, F32)),
        (pos, mixed, hidden, slope, *pieces, w_second),
        [SMEM] + [VMEM] * 8,
        [pltpu.VMEM((SPAN, channels), BF16)],
    )


def place_body(pos, *refs):
    mine, other, (first, second) = refs[:QUAD], refs[QUAD : 2 * QUAD], refs[2 * QUAD :]
    keeps_first = (pos[0] & 1) == 0

    def fill(mine_out, other_out):
        for p in range(QUAD):
            share = lanes_of(chip(pos) ^ p)
            mine_out[:, share] = mine[p][...].astype(F32)
            other_out[:, share] = other[p][...].astype(F32)

    @pl.when(keeps_first)
    def _():
        fill(first, second)

    @pl.when(jnp.logical_not(keeps_first))
    def _():
        fill(second, first)


def place(pos, mine, other):
    channels = mine[0].shape[0]
    return call(
        place_body,
        (shaped(channels, channels, F32),) * 2,
        (pos, *mine, *other),
        [SMEM] + [VMEM] * (2 * QUAD),
    )


def planned_shards(
    features,
    tile_entries,
    tile_columns,
    tiles_per_row,
    rev_vals,
    rev_cols,
    rev_count,
    w_first,
    w_second,
    cotangent,
):
    pos = lax.axis_index(AXES).astype(jnp.int32).reshape(1)
    *packed, both_tiles = pack(
        pos,
        tile_columns,
        tiles_per_row,
        rev_cols,
        rev_count,
        features,
        cotangent,
        tile_entries,
        rev_vals,
    )
    parts = [packed[0]] + [swap(packed[q], 2 * q) for q in range(1, QUAD)]
    share, places = unpack(pos, parts)
    tiles = over_quad(both_tiles)

    def everywhere(own):
        planes = over_planes(own)
        return planes + [swap(plane, CORE) for plane in planes]

    shares = everywhere(share)
    (mixed_share,) = mix(places, 0, 0, shares, tiles)
    (spread_share,) = mix(places, 2, 1, shares, tiles)
    mixed, hidden, hidden_share, slope = first_layer(pos, over_quad(mixed_share), w_first)
    again = mix(places, 0, 0, everywhere(hidden_share), tiles, split=True)
    z_out = second_layer(
        pos, [again[0]] + [swap(again[q], 2 * q) for q in range(1, QUAD)], w_second
    )
    keep, send = gradients(pos, mixed, hidden, slope, over_quad(spread_share), w_second)
    total = (keep + swap(send, CORE)).astype(BF16)
    for mask in (8, 16):
        total = (total.astype(F32) + swap(total, mask).astype(F32)).astype(BF16)
    mine = over_quad(total)
    grad_first, grad_second = place(pos, mine, [swap(piece, CORE) for piece in mine])
    return (z_out, grad_first, grad_second)


def solution(mesh):
    placed = (
        P(AXES, None),
        P(AXES, None, None),
        P(AXES, None),
        P(AXES),
        P(AXES, None, None),
        P(AXES, None),
        P(AXES),
        P(),
        P(),
        P(AXES, None),
    )
    planned = mesh.shape["rows"] == 8 and mesh.shape["grp"] == 4
    return jax.shard_map(
        planned_shards if planned else gathered_shards,
        mesh=mesh,
        in_specs=placed,
        out_specs=(P(AXES, None), P(), P()),
        check_vma=False,
    )
```

```python
import functools

import jax
import jax.numpy as jnp
from jax import lax
from jax.experimental import pallas as pl
from jax.experimental.pallas import tpu as pltpu
from jax.sharding import PartitionSpec as P

AXES = ("rows", "grp")
F32 = jnp.float32
BF16 = jnp.bfloat16


def aggregate(panel_vals, strip_columns, strip_count, everyone, own_rows):
    blocks, size_block, span_width = panel_vals.shape
    slot_count = span_width // size_block
    channels = everyone.shape[1]
    block_table = everyone.reshape(-1, size_block, channels)
    slot_ids = lax.broadcasted_iota(jnp.int32, strip_columns.shape, 1)
    weights = (slot_ids < strip_count[:, None]).astype(everyone.dtype)
    picked = (block_table[strip_columns] * weights[:, :, None, None]).reshape(
        blocks, slot_count * size_block, channels
    )
    summed_rows = jnp.einsum("bik,bkc->bic", panel_vals, picked, preferred_element_type=F32)
    return summed_rows.reshape(blocks * size_block, channels) + own_rows.astype(F32)


def gathered_shards(
    features,
    tile_entries,
    tile_columns,
    tiles_per_row,
    rev_vals,
    rev_cols,
    rev_count,
    w_first,
    w_second,
    cotangent,
):
    channels = features.shape[1]
    pair = jnp.concatenate([features, cotangent], axis=1)
    pair_all = lax.all_gather(pair, AXES, axis=0, tiled=True)
    mixed_own = aggregate(
        tile_entries, tile_columns, tiles_per_row, pair_all[:, :channels], features
    ).astype(BF16)
    spread_own = aggregate(
        rev_vals, rev_cols, rev_count, pair_all[:, channels:], cotangent
    ).astype(BF16)
    both_all = lax.all_gather(
        jnp.concatenate([mixed_own, spread_own], axis=1), AXES, axis=0, tiled=True
    )
    mixed = both_all[:, :channels]
    spread = both_all[:, channels:]
    pre_first = jnp.dot(mixed, w_first, preferred_element_type=F32)
    sig = jax.nn.sigmoid(pre_first)
    hidden = (pre_first * sig).astype(BF16)
    slope = sig * (1.0 + pre_first * (1.0 - sig))
    back_hidden = lax.dot_general(
        spread, w_second, (((1,), (1,)), ((), ())), preferred_element_type=F32
    )
    back_first = (back_hidden * slope).astype(BF16)
    grad_first = lax.dot_general(
        mixed, back_first, (((0,), (0,)), ((), ())), preferred_element_type=F32
    )
    grad_second = lax.dot_general(
        hidden, spread, (((0,), (0,)), ((), ())), preferred_element_type=F32
    )
    position = lax.axis_index(AXES) * features.shape[0]
    hidden_own = lax.dynamic_slice_in_dim(hidden, position, features.shape[0], 0)
    mixed_second = aggregate(
        tile_entries, tile_columns, tiles_per_row, hidden, hidden_own
    ).astype(BF16)
    z_out = jnp.dot(mixed_second, w_second, preferred_element_type=F32).astype(BF16)
    return (z_out, grad_first, grad_second)


CORE = 1
DEVICES, QUAD, PLANES, SLOTS, BLOCK = 32, 4, 4, 16, 64
LANES = 128
ROWS = 128
SPAN = QUAD * ROWS
VMEM = pl.BlockSpec(memory_space=pltpu.VMEM)
SMEM = pl.BlockSpec(memory_space=pltpu.SMEM)
HBM = pl.BlockSpec(memory_space=pltpu.HBM)
PARAMS = pltpu.CompilerParams(vmem_limit_bytes=48 * 1024 * 1024)


def call(body, out_shape, operands, spaces, scratch=()):
    return pl.pallas_call(
        body,
        out_shape=out_shape,
        in_specs=list(spaces),
        out_specs=jax.tree.map(lambda _: VMEM, out_shape),
        scratch_shapes=list(scratch),
        compiler_params=PARAMS,
    )(*operands)


def shaped(rows, columns, dtype=BF16):
    return jax.ShapeDtypeStruct((rows, columns), dtype)


def swap(value, mask):
    return lax.ppermute(value, AXES, [(i, i ^ mask) for i in range(DEVICES)])


def over_quad(value):
    return [value] + [swap(value, 2 * q) for q in range(1, QUAD)]


def over_planes(value):
    second = swap(value, 16)
    return [value, swap(value, 8), second, swap(second, 8)]


def chip(pos):
    return (pos[0] >> 1) & 3


def lanes_of(column):
    return pl.ds(pl.multiple_of(column * LANES, LANES), LANES)


def pack_body(pos, *refs):
    tables, (features, cotangent, tiles, back_tiles) = refs[:4], refs[4:8]
    outs, both_tiles, scalars, sems = refs[8:12], refs[12], refs[13:17], refs[17]
    copies = [(table, scalar) for table, scalar in zip(tables, scalars)]
    for q, out in enumerate(outs):
        share = lanes_of(chip(pos) ^ q)
        copies.append((features.at[:, share], out.at[pl.ds(0, ROWS), pl.ds(0, LANES)]))
        copies.append((cotangent.at[:, share], out.at[pl.ds(0, ROWS), pl.ds(LANES, LANES)]))
    copies.append((tiles, both_tiles.at[pl.ds(0, 2)]))
    copies.append((back_tiles, both_tiles.at[pl.ds(2, 2)]))
    copies = [pltpu.make_async_copy(a, b, sems.at[i]) for i, (a, b) in enumerate(copies)]
    for copy in copies:
        copy.start()
    for copy in copies[:4]:
        copy.wait()
    line = lax.broadcasted_iota(jnp.int32, (16, LANES), 0)
    lane = lax.broadcasted_iota(jnp.int32, (16, LANES), 1)
    codes = jnp.full((16, LANES), -1, jnp.int32)
    for r in range(2):
        table, count = scalars[2 * r], scalars[2 * r + 1]
        for w in range(2):
            for s in range(SLOTS):
                value = jnp.where(s < count[w], table[w, s], -1)
                codes = jnp.where((line == 2 * r + w) & (lane == s), value, codes)
    codes = codes.astype(F32).astype(BF16)
    for out in outs:
        out[ROWS:, :LANES] = codes
        out[ROWS:, LANES:] = codes
    for copy in copies[4:]:
        copy.wait()


def pack(pos, columns, counts, back_columns, back_counts, features, cotangent, tiles, back_tiles):
    return call(
        pack_body,
        (shaped(ROWS + 16, 2 * LANES),) * QUAD
        + (jax.ShapeDtypeStruct((4, BLOCK, SLOTS * BLOCK), BF16),),
        (pos, columns, counts, back_columns, back_counts, features, cotangent, tiles, back_tiles),
        [SMEM] + [HBM] * 8,
        [pltpu.SMEM((2, SLOTS), jnp.int32), pltpu.SMEM((2,), jnp.int32)] * 2
        + [pltpu.SemaphoreType.DMA((14,))],
    )


def unpack_body(pos, *refs):
    parts, (both, places) = refs[:QUAD], refs[QUAD:]
    for q, part in enumerate(parts):
        both[pl.ds(q * ROWS, ROWS), :] = part[:ROWS, :]
        block = part[ROWS:, :LANES].astype(F32).astype(jnp.int32)
        apart = (block >> 1) ^ pos[0]
        place = ((apart & 1) * 16 + (apart >> 3) * 4 + ((apart >> 1) & 3)) * 2 + (block & 1)
        place = jnp.where(block < 0, 2 * DEVICES, place)
        places[q * 8 : q * 8 + 8, :] = place[:8, :]


def unpack(pos, parts):
    return call(
        unpack_body,
        (shaped(SPAN, 2 * LANES), shaped(8 * QUAD, LANES, jnp.int32)),
        (pos, *parts),
        [SMEM] + [VMEM] * QUAD,
    )


def mix_rows(base, half, places, shares, tiles, table, picked, store):
    for i, share in enumerate(shares):
        table[pl.ds(i * SPAN, SPAN), :] = share[:, pl.ds(half * LANES, LANES)]
    table[DEVICES * ROWS :, :] = jnp.zeros((BLOCK, LANES), BF16)
    for q in range(QUAD):
        for w in range(2):
            row = q * 2 + w
            for s in range(SLOTS):
                first = pl.multiple_of(places[q * 8 + base + w, s] * BLOCK, BLOCK)
                picked[row, pl.ds(s * BLOCK, BLOCK), :] = table[pl.ds(first, BLOCK), :]
            total = jnp.dot(tiles[q][base + w], picked[row], preferred_element_type=F32)
            total = total + table[pl.ds(row * BLOCK, BLOCK), :].astype(F32)
            store(q, w, total.astype(BF16))


MIX_SCRATCH = (
    pltpu.VMEM((DEVICES * ROWS + BLOCK, LANES), BF16),
    pltpu.VMEM((2 * QUAD, SLOTS * BLOCK, LANES), BF16),
)


def mix_body(base, half, places, *refs):
    shares, tiles, (out, table, picked) = refs[:8], refs[8:12], refs[12:]

    def store(q, w, rows):
        out[pl.ds(q * ROWS + w * BLOCK, BLOCK), :] = rows

    mix_rows(base, half, places, shares, tiles, table, picked, store)


def mix(places, base, half, shares, tiles):
    return call(
        functools.partial(mix_body, base, half),
        shaped(SPAN, LANES),
        (places, *shares, *tiles),
        [SMEM] + [VMEM] * 12,
        MIX_SCRATCH,
    )


def mix_beside_body(places, *refs):
    shares, tiles, total = refs[:8], refs[8:12], refs[12]
    outs, (table, picked) = refs[13:17], refs[17:]
    extent = total.shape[0]
    for out in outs:
        out[:extent, :] = total[...]

    def store(q, w, rows):
        outs[q][pl.ds(extent + w * BLOCK, BLOCK), :] = rows

    mix_rows(0, 0, places, shares, tiles, table, picked, store)


def mix_beside(places, shares, tiles, total):
    return call(
        mix_beside_body,
        (shaped(total.shape[0] + ROWS, LANES),) * QUAD,
        (places, *shares, *tiles, total),
        [SMEM] + [VMEM] * 13,
        MIX_SCRATCH,
    )


def whole_rows(pos, pieces, target):
    for p, piece in enumerate(pieces):
        share = lanes_of(chip(pos) ^ p)
        for q in range(QUAD):
            target[pl.ds(q * ROWS, ROWS), share] = piece[pl.ds((p ^ q) * ROWS, ROWS), :]


def first_body(pos, p0, p1, p2, p3, w_first, mixed, hidden, hidden_share, slope, full):
    whole_rows(pos, (p0, p1, p2, p3), mixed)
    pre = jnp.dot(mixed[...], w_first[...], preferred_element_type=F32)
    sig = jax.nn.sigmoid(pre)
    hidden[...] = (pre * sig).astype(BF16)
    full[...] = sig * (1.0 + pre * (1.0 - sig))
    share = lanes_of(chip(pos))
    hidden_share[...] = hidden[:, share]
    slope[...] = full[:, share]


def first_layer(pos, pieces, w_first):
    channels = w_first.shape[0]
    return call(
        first_body,
        (
            shaped(SPAN, channels),
            shaped(SPAN, channels),
            shaped(SPAN, LANES),
            shaped(SPAN, LANES, F32),
        ),
        (pos, *pieces, w_first),
        [SMEM] + [VMEM] * 5,
        [pltpu.VMEM((SPAN, channels), F32)],
    )


def second_body(pos, p0, p1, p2, p3, w_second, z_out):
    total = jnp.zeros(z_out.shape, F32)
    for p, piece in enumerate((p0, p1, p2, p3)):
        total = total + jnp.dot(
            piece[piece.shape[0] - ROWS :, :],
            w_second[lanes_of(chip(pos) ^ p), :],
            preferred_element_type=F32,
        )
    z_out[...] = total.astype(BF16)


def second_layer(pos, pieces, w_second):
    return call(
        second_body,
        shaped(ROWS, w_second.shape[0]),
        (pos, *pieces, w_second),
        [SMEM] + [VMEM] * 5,
    )


def grads_body(pos, mixed, hidden, slope, p0, p1, p2, p3, w_second, keep, send, spread):
    whole_rows(pos, (p0, p1, p2, p3), spread)
    back_hidden = lax.dot_general(
        spread[...],
        w_second[lanes_of(chip(pos)), :],
        (((1,), (1,)), ((), ())),
        preferred_element_type=F32,
    )
    back_first = (back_hidden * slope[...]).astype(BF16)
    over_rows = (((0,), (0,)), ((), ()))
    first = lax.dot_general(mixed[...], back_first, over_rows, preferred_element_type=F32)
    second = lax.dot_general(hidden[...], p0[...], over_rows, preferred_element_type=F32)
    keeps_first = (pos[0] & 1) == 0

    @pl.when(keeps_first)
    def _():
        keep[...] = first
        send[...] = second

    @pl.when(jnp.logical_not(keeps_first))
    def _():
        keep[...] = second
        send[...] = first


def gradients(pos, mixed, hidden, slope, pieces, w_second):
    channels = w_second.shape[0]
    return call(
        grads_body,
        (shaped(channels, LANES, F32), shaped(channels, LANES, F32)),
        (pos, mixed, hidden, slope, *pieces, w_second),
        [SMEM] + [VMEM] * 8,
        [pltpu.VMEM((SPAN, channels), BF16)],
    )


def place_body(pos, *refs):
    mine, other, (first, second) = refs[:QUAD], refs[QUAD : 2 * QUAD], refs[2 * QUAD :]
    extent = first.shape[0]
    keeps_first = (pos[0] & 1) == 0

    def fill(mine_out, other_out):
        for p in range(QUAD):
            share = lanes_of(chip(pos) ^ p)
            mine_out[:, share] = mine[p][:extent, :].astype(F32)
            other_out[:, share] = other[p][:extent, :].astype(F32)

    @pl.when(keeps_first)
    def _():
        fill(first, second)

    @pl.when(jnp.logical_not(keeps_first))
    def _():
        fill(second, first)


def place(pos, mine, other):
    channels = QUAD * LANES
    return call(
        place_body,
        (shaped(channels, channels, F32),) * 2,
        (pos, *mine, *other),
        [SMEM] + [VMEM] * (2 * QUAD),
    )


def planned_shards(
    features,
    tile_entries,
    tile_columns,
    tiles_per_row,
    rev_vals,
    rev_cols,
    rev_count,
    w_first,
    w_second,
    cotangent,
):
    pos = lax.axis_index(AXES).astype(jnp.int32).reshape(1)
    *packed, both_tiles = pack(
        pos,
        tile_columns,
        tiles_per_row,
        rev_cols,
        rev_count,
        features,
        cotangent,
        tile_entries,
        rev_vals,
    )
    parts = [packed[0]] + [swap(packed[q], 2 * q) for q in range(1, QUAD)]
    share, places = unpack(pos, parts)
    tiles = over_quad(both_tiles)

    def everywhere(own):
        planes = over_planes(own)
        return planes + [swap(plane, CORE) for plane in planes]

    shares = everywhere(share)
    mixed_share = mix(places, 0, 0, shares, tiles)
    spread_share = mix(places, 2, 1, shares, tiles)
    mixed, hidden, hidden_share, slope = first_layer(pos, over_quad(mixed_share), w_first)
    keep, send = gradients(pos, mixed, hidden, slope, over_quad(spread_share), w_second)
    total = (keep + swap(send, CORE)).astype(BF16)
    for mask in (8, 16):
        total = (total.astype(F32) + swap(total, mask).astype(F32)).astype(BF16)
    beside = mix_beside(places, everywhere(hidden_share), tiles, total)
    mine = [beside[0]] + [swap(beside[q], 2 * q) for q in range(1, QUAD)]
    z_out = second_layer(pos, mine, w_second)
    grad_first, grad_second = place(pos, mine, [swap(piece, CORE) for piece in mine])
    return (z_out, grad_first, grad_second)


def solution(mesh):
    placed = (
        P(AXES, None),
        P(AXES, None, None),
        P(AXES, None),
        P(AXES),
        P(AXES, None, None),
        P(AXES, None),
        P(AXES),
        P(),
        P(),
        P(AXES, None),
    )
    planned = mesh.shape["rows"] == 8 and mesh.shape["grp"] == 4
    return jax.shard_map(
        planned_shards if planned else gathered_shards,
        mesh=mesh,
        in_specs=placed,
        out_specs=(P(AXES, None), P(), P()),
        check_vma=False,
    )
```

```python
import functools

import jax
import jax.numpy as jnp
from jax import lax
from jax.experimental import pallas as pl
from jax.experimental.pallas import tpu as pltpu
from jax.sharding import PartitionSpec as P

AXES = ("rows", "grp")
F32 = jnp.float32
BF16 = jnp.bfloat16


def aggregate(panel_vals, strip_columns, strip_count, everyone, own_rows):
    blocks, size_block, span_width = panel_vals.shape
    slot_count = span_width // size_block
    channels = everyone.shape[1]
    block_table = everyone.reshape(-1, size_block, channels)
    slot_ids = lax.broadcasted_iota(jnp.int32, strip_columns.shape, 1)
    weights = (slot_ids < strip_count[:, None]).astype(everyone.dtype)
    picked = (block_table[strip_columns] * weights[:, :, None, None]).reshape(
        blocks, slot_count * size_block, channels
    )
    summed_rows = jnp.einsum("bik,bkc->bic", panel_vals, picked, preferred_element_type=F32)
    return summed_rows.reshape(blocks * size_block, channels) + own_rows.astype(F32)


def gathered_shards(
    features,
    tile_entries,
    tile_columns,
    tiles_per_row,
    rev_vals,
    rev_cols,
    rev_count,
    w_first,
    w_second,
    cotangent,
):
    channels = features.shape[1]
    pair = jnp.concatenate([features, cotangent], axis=1)
    pair_all = lax.all_gather(pair, AXES, axis=0, tiled=True)
    mixed_own = aggregate(
        tile_entries, tile_columns, tiles_per_row, pair_all[:, :channels], features
    ).astype(BF16)
    spread_own = aggregate(
        rev_vals, rev_cols, rev_count, pair_all[:, channels:], cotangent
    ).astype(BF16)
    both_all = lax.all_gather(
        jnp.concatenate([mixed_own, spread_own], axis=1), AXES, axis=0, tiled=True
    )
    mixed = both_all[:, :channels]
    spread = both_all[:, channels:]
    pre_first = jnp.dot(mixed, w_first, preferred_element_type=F32)
    sig = jax.nn.sigmoid(pre_first)
    hidden = (pre_first * sig).astype(BF16)
    slope = sig * (1.0 + pre_first * (1.0 - sig))
    back_hidden = lax.dot_general(
        spread, w_second, (((1,), (1,)), ((), ())), preferred_element_type=F32
    )
    back_first = (back_hidden * slope).astype(BF16)
    grad_first = lax.dot_general(
        mixed, back_first, (((0,), (0,)), ((), ())), preferred_element_type=F32
    )
    grad_second = lax.dot_general(
        hidden, spread, (((0,), (0,)), ((), ())), preferred_element_type=F32
    )
    position = lax.axis_index(AXES) * features.shape[0]
    hidden_own = lax.dynamic_slice_in_dim(hidden, position, features.shape[0], 0)
    mixed_second = aggregate(
        tile_entries, tile_columns, tiles_per_row, hidden, hidden_own
    ).astype(BF16)
    z_out = jnp.dot(mixed_second, w_second, preferred_element_type=F32).astype(BF16)
    return (z_out, grad_first, grad_second)


CORE = 1
DEVICES, QUAD, PLANES, SLOTS, BLOCK = 32, 4, 4, 16, 64
LANES = 128
ROWS = 128
SPAN = QUAD * ROWS
VMEM = pl.BlockSpec(memory_space=pltpu.VMEM)
SMEM = pl.BlockSpec(memory_space=pltpu.SMEM)
HBM = pl.BlockSpec(memory_space=pltpu.HBM)
PARAMS = pltpu.CompilerParams(vmem_limit_bytes=48 * 1024 * 1024)


def call(body, out_shape, operands, spaces, scratch=()):
    return pl.pallas_call(
        body,
        out_shape=out_shape,
        in_specs=list(spaces),
        out_specs=jax.tree.map(lambda _: VMEM, out_shape),
        scratch_shapes=list(scratch),
        compiler_params=PARAMS,
    )(*operands)


def shaped(rows, columns, dtype=BF16):
    return jax.ShapeDtypeStruct((rows, columns), dtype)


def swap(value, mask):
    return lax.ppermute(value, AXES, [(i, i ^ mask) for i in range(DEVICES)])


def over_quad(value):
    return [value] + [swap(value, 2 * q) for q in range(1, QUAD)]


def over_planes(value):
    second = swap(value, 16)
    return [value, swap(value, 8), second, swap(second, 8)]


def chip(pos):
    return (pos[0] >> 1) & 3


def lanes_of(column):
    return pl.ds(pl.multiple_of(column * LANES, LANES), LANES)


def pack_body(pos, *refs):
    tables, (features, cotangent, tiles, back_tiles) = refs[:4], refs[4:8]
    outs, both_tiles, scalars, sems = refs[8:12], refs[12], refs[13:17], refs[17]
    copies = [(table, scalar) for table, scalar in zip(tables, scalars)]
    for q, out in enumerate(outs):
        share = lanes_of(chip(pos) ^ q)
        copies.append((features.at[:, share], out.at[pl.ds(0, ROWS), pl.ds(0, LANES)]))
        copies.append((cotangent.at[:, share], out.at[pl.ds(0, ROWS), pl.ds(LANES, LANES)]))
    copies.append((tiles, both_tiles.at[pl.ds(0, 2)]))
    copies.append((back_tiles, both_tiles.at[pl.ds(2, 2)]))
    copies = [pltpu.make_async_copy(a, b, sems.at[i]) for i, (a, b) in enumerate(copies)]
    for copy in copies:
        copy.start()
    for copy in copies[:4]:
        copy.wait()
    line = lax.broadcasted_iota(jnp.int32, (16, LANES), 0)
    lane = lax.broadcasted_iota(jnp.int32, (16, LANES), 1)
    codes = jnp.full((16, LANES), -1, jnp.int32)
    for r in range(2):
        table, count = scalars[2 * r], scalars[2 * r + 1]
        for w in range(2):
            for s in range(SLOTS):
                value = jnp.where(s < count[w], table[w, s], -1)
                codes = jnp.where((line == 2 * r + w) & (lane == s), value, codes)
    codes = codes.astype(F32).astype(BF16)
    for out in outs:
        out[ROWS:, :LANES] = codes
        out[ROWS:, LANES:] = codes
    for copy in copies[4:]:
        copy.wait()


def pack(pos, columns, counts, back_columns, back_counts, features, cotangent, tiles, back_tiles):
    return call(
        pack_body,
        (shaped(ROWS + 16, 2 * LANES),) * QUAD
        + (jax.ShapeDtypeStruct((4, BLOCK, SLOTS * BLOCK), BF16),),
        (pos, columns, counts, back_columns, back_counts, features, cotangent, tiles, back_tiles),
        [SMEM] + [HBM] * 8,
        [pltpu.SMEM((2, SLOTS), jnp.int32), pltpu.SMEM((2,), jnp.int32)] * 2
        + [pltpu.SemaphoreType.DMA((14,))],
    )


def unpack_body(pos, *refs):
    parts, (both, places) = refs[:QUAD], refs[QUAD:]
    for q, part in enumerate(parts):
        both[pl.ds(q * ROWS, ROWS), :] = part[:ROWS, :]
        block = part[ROWS:, :LANES].astype(F32).astype(jnp.int32)
        apart = (block >> 1) ^ pos[0]
        place = ((apart & 1) * 16 + (apart >> 3) * 4 + ((apart >> 1) & 3)) * 2 + (block & 1)
        place = jnp.where(block < 0, 2 * DEVICES, place)
        places[q * 8 : q * 8 + 8, :] = place[:8, :]


def unpack(pos, parts):
    return call(
        unpack_body,
        (shaped(SPAN, 2 * LANES), shaped(8 * QUAD, LANES, jnp.int32)),
        (pos, *parts),
        [SMEM] + [VMEM] * QUAD,
    )


def mix_rows(base, half, places, shares, tiles, table, picked, store):
    for i, share in enumerate(shares):
        table[pl.ds(i * SPAN, SPAN), :] = share[:, pl.ds(half * LANES, LANES)]
    table[DEVICES * ROWS :, :] = jnp.zeros((BLOCK, LANES), BF16)
    for q in range(QUAD):
        for w in range(2):
            row = q * 2 + w
            for s in range(SLOTS):
                first = pl.multiple_of(places[q * 8 + base + w, s] * BLOCK, BLOCK)
                picked[row, pl.ds(s * BLOCK, BLOCK), :] = table[pl.ds(first, BLOCK), :]
            total = jnp.dot(tiles[q][base + w], picked[row], preferred_element_type=F32)
            total = total + table[pl.ds(row * BLOCK, BLOCK), :].astype(F32)
            store(q, w, total.astype(BF16))


MIX_SCRATCH = (
    pltpu.VMEM((DEVICES * ROWS + BLOCK, LANES), BF16),
    pltpu.VMEM((2 * QUAD, SLOTS * BLOCK, LANES), BF16),
)


def mix_body(base, half, places, *refs):
    shares, tiles, (out, table, picked) = refs[:8], refs[8:12], refs[12:]

    def store(q, w, rows):
        out[pl.ds(q * ROWS + w * BLOCK, BLOCK), :] = rows

    mix_rows(base, half, places, shares, tiles, table, picked, store)


def mix(places, base, half, shares, tiles):
    return call(
        functools.partial(mix_body, base, half),
        shaped(SPAN, LANES),
        (places, *shares, *tiles),
        [SMEM] + [VMEM] * 12,
        MIX_SCRATCH,
    )


def mix_beside_body(places, *refs):
    shares, tiles, total = refs[:8], refs[8:12], refs[12]
    outs, (table, picked) = refs[13:17], refs[17:]
    extent = total.shape[0]
    for out in outs:
        out[:extent, :] = total[...]

    def store(q, w, rows):
        outs[q][pl.ds(extent + w * BLOCK, BLOCK), :] = rows

    mix_rows(0, 0, places, shares, tiles, table, picked, store)


def mix_beside(places, shares, tiles, total):
    return call(
        mix_beside_body,
        (shaped(total.shape[0] + ROWS, LANES),) * QUAD,
        (places, *shares, *tiles, total),
        [SMEM] + [VMEM] * 13,
        MIX_SCRATCH,
    )


def whole_rows(pos, pieces, target):
    for p, piece in enumerate(pieces):
        share = lanes_of(chip(pos) ^ p)
        for q in range(QUAD):
            target[pl.ds(q * ROWS, ROWS), share] = piece[pl.ds((p ^ q) * ROWS, ROWS), :]


def first_body(pos, p0, p1, p2, p3, w_first, mixed, hidden, hidden_share, slope, full):
    whole_rows(pos, (p0, p1, p2, p3), mixed)
    pre = jnp.dot(mixed[...], w_first[...], preferred_element_type=F32)
    sig = jax.nn.sigmoid(pre)
    hidden[...] = (pre * sig).astype(BF16)
    full[...] = sig * (1.0 + pre * (1.0 - sig))
    share = lanes_of(chip(pos))
    hidden_share[...] = hidden[:, share]
    slope[...] = full[:, share]


def first_layer(pos, pieces, w_first):
    channels = w_first.shape[0]
    return call(
        first_body,
        (
            shaped(SPAN, channels),
            shaped(SPAN, channels),
            shaped(SPAN, LANES),
            shaped(SPAN, LANES, F32),
        ),
        (pos, *pieces, w_first),
        [SMEM] + [VMEM] * 5,
        [pltpu.VMEM((SPAN, channels), F32)],
    )


def second_body(pos, p0, p1, p2, p3, w_second, z_out):
    total = jnp.zeros(z_out.shape, F32)
    for p, piece in enumerate((p0, p1, p2, p3)):
        total = total + jnp.dot(
            piece[piece.shape[0] - ROWS :, :],
            w_second[lanes_of(chip(pos) ^ p), :],
            preferred_element_type=F32,
        )
    z_out[...] = total.astype(BF16)


def second_layer(pos, pieces, w_second):
    return call(
        second_body,
        shaped(ROWS, w_second.shape[0]),
        (pos, *pieces, w_second),
        [SMEM] + [VMEM] * 5,
    )


def grads_body(pos, mixed, hidden, slope, p0, p1, p2, p3, w_second, keep, send, spread):
    whole_rows(pos, (p0, p1, p2, p3), spread)
    back_hidden = lax.dot_general(
        spread[...],
        w_second[lanes_of(chip(pos)), :],
        (((1,), (1,)), ((), ())),
        preferred_element_type=F32,
    )
    back_first = (back_hidden * slope[...]).astype(BF16)
    over_rows = (((0,), (0,)), ((), ()))
    first = lax.dot_general(mixed[...], back_first, over_rows, preferred_element_type=F32)
    second = lax.dot_general(hidden[...], p0[...], over_rows, preferred_element_type=F32)
    keeps_first = (pos[0] & 1) == 0

    @pl.when(keeps_first)
    def _():
        keep[...] = first
        send[...] = second

    @pl.when(jnp.logical_not(keeps_first))
    def _():
        keep[...] = second
        send[...] = first


def gradients(pos, mixed, hidden, slope, pieces, w_second):
    channels = w_second.shape[0]
    return call(
        grads_body,
        (shaped(channels, LANES, F32), shaped(channels, LANES, F32)),
        (pos, mixed, hidden, slope, *pieces, w_second),
        [SMEM] + [VMEM] * 8,
        [pltpu.VMEM((SPAN, channels), BF16)],
    )


def place_body(pos, *refs):
    mine, other, (first, second) = refs[:QUAD], refs[QUAD : 2 * QUAD], refs[2 * QUAD :]
    extent = first.shape[0]
    keeps_first = (pos[0] & 1) == 0

    def fill(mine_out, other_out):
        for p in range(QUAD):
            share = lanes_of(chip(pos) ^ p)
            mine_out[:, share] = mine[p][:extent, :].astype(F32)
            other_out[:, share] = other[p][:extent, :].astype(F32)

    @pl.when(keeps_first)
    def _():
        fill(first, second)

    @pl.when(jnp.logical_not(keeps_first))
    def _():
        fill(second, first)


def place(pos, mine, other):
    channels = QUAD * LANES
    return call(
        place_body,
        (shaped(channels, channels, F32),) * 2,
        (pos, *mine, *other),
        [SMEM] + [VMEM] * (2 * QUAD),
    )


def planned_shards(
    features,
    tile_entries,
    tile_columns,
    tiles_per_row,
    rev_vals,
    rev_cols,
    rev_count,
    w_first,
    w_second,
    cotangent,
):
    pos = lax.axis_index(AXES).astype(jnp.int32).reshape(1)
    operands = (
        tile_columns,
        tiles_per_row,
        rev_cols,
        rev_count,
        features,
        cotangent,
        tile_entries,
        rev_vals,
    )
    operands = [pltpu.with_memory_space_constraint(value, pltpu.HBM) for value in operands]
    *packed, both_tiles = pack(pos, *operands)
    parts = [packed[0]] + [swap(packed[q], 2 * q) for q in range(1, QUAD)]
    share, places = unpack(pos, parts)
    tiles = over_quad(both_tiles)

    def everywhere(own):
        planes = over_planes(own)
        return planes + [swap(plane, CORE) for plane in planes]

    shares = everywhere(share)
    mixed_share = mix(places, 0, 0, shares, tiles)
    spread_share = mix(places, 2, 1, shares, tiles)
    mixed, hidden, hidden_share, slope = first_layer(pos, over_quad(mixed_share), w_first)
    keep, send = gradients(pos, mixed, hidden, slope, over_quad(spread_share), w_second)
    total = (keep + swap(send, CORE)).astype(BF16)
    for mask in (8, 16):
        total = (total.astype(F32) + swap(total, mask).astype(F32)).astype(BF16)
    beside = mix_beside(places, everywhere(hidden_share), tiles, total)
    mine = [beside[0]] + [swap(beside[q], 2 * q) for q in range(1, QUAD)]
    z_out = second_layer(pos, mine, w_second)
    grad_first, grad_second = place(pos, mine, [swap(piece, CORE) for piece in mine])
    return (z_out, grad_first, grad_second)


def solution(mesh):
    placed = (
        P(AXES, None),
        P(AXES, None, None),
        P(AXES, None),
        P(AXES),
        P(AXES, None, None),
        P(AXES, None),
        P(AXES),
        P(),
        P(),
        P(AXES, None),
    )
    planned = mesh.shape["rows"] == 8 and mesh.shape["grp"] == 4
    return jax.shard_map(
        planned_shards if planned else gathered_shards,
        mesh=mesh,
        in_specs=placed,
        out_specs=(P(AXES, None), P(), P()),
        check_vma=False,
    )
```

```python
import functools

import jax
import jax.numpy as jnp
from jax import lax
from jax.experimental import pallas as pl
from jax.experimental.pallas import tpu as pltpu
from jax.sharding import PartitionSpec as P

AXES = ("rows", "grp")
F32 = jnp.float32
BF16 = jnp.bfloat16


def aggregate(panel_vals, strip_columns, strip_count, everyone, own_rows):
    blocks, size_block, span_width = panel_vals.shape
    slot_count = span_width // size_block
    channels = everyone.shape[1]
    block_table = everyone.reshape(-1, size_block, channels)
    slot_ids = lax.broadcasted_iota(jnp.int32, strip_columns.shape, 1)
    weights = (slot_ids < strip_count[:, None]).astype(everyone.dtype)
    picked = (block_table[strip_columns] * weights[:, :, None, None]).reshape(
        blocks, slot_count * size_block, channels
    )
    summed_rows = jnp.einsum("bik,bkc->bic", panel_vals, picked, preferred_element_type=F32)
    return summed_rows.reshape(blocks * size_block, channels) + own_rows.astype(F32)


def gathered_shards(
    features,
    tile_entries,
    tile_columns,
    tiles_per_row,
    rev_vals,
    rev_cols,
    rev_count,
    w_first,
    w_second,
    cotangent,
):
    channels = features.shape[1]
    pair = jnp.concatenate([features, cotangent], axis=1)
    pair_all = lax.all_gather(pair, AXES, axis=0, tiled=True)
    mixed_own = aggregate(
        tile_entries, tile_columns, tiles_per_row, pair_all[:, :channels], features
    ).astype(BF16)
    spread_own = aggregate(
        rev_vals, rev_cols, rev_count, pair_all[:, channels:], cotangent
    ).astype(BF16)
    both_all = lax.all_gather(
        jnp.concatenate([mixed_own, spread_own], axis=1), AXES, axis=0, tiled=True
    )
    mixed = both_all[:, :channels]
    spread = both_all[:, channels:]
    pre_first = jnp.dot(mixed, w_first, preferred_element_type=F32)
    sig = jax.nn.sigmoid(pre_first)
    hidden = (pre_first * sig).astype(BF16)
    slope = sig * (1.0 + pre_first * (1.0 - sig))
    back_hidden = lax.dot_general(
        spread, w_second, (((1,), (1,)), ((), ())), preferred_element_type=F32
    )
    back_first = (back_hidden * slope).astype(BF16)
    grad_first = lax.dot_general(
        mixed, back_first, (((0,), (0,)), ((), ())), preferred_element_type=F32
    )
    grad_second = lax.dot_general(
        hidden, spread, (((0,), (0,)), ((), ())), preferred_element_type=F32
    )
    position = lax.axis_index(AXES) * features.shape[0]
    hidden_own = lax.dynamic_slice_in_dim(hidden, position, features.shape[0], 0)
    mixed_second = aggregate(
        tile_entries, tile_columns, tiles_per_row, hidden, hidden_own
    ).astype(BF16)
    z_out = jnp.dot(mixed_second, w_second, preferred_element_type=F32).astype(BF16)
    return (z_out, grad_first, grad_second)


CORE = 1
DEVICES, QUAD, PLANES, SLOTS, BLOCK = 32, 4, 4, 16, 64
LANES = 128
ROWS = 128
SPAN = QUAD * ROWS
VMEM = pl.BlockSpec(memory_space=pltpu.VMEM)
SMEM = pl.BlockSpec(memory_space=pltpu.SMEM)
HBM = pl.BlockSpec(memory_space=pltpu.HBM)
PARAMS = pltpu.CompilerParams(vmem_limit_bytes=48 * 1024 * 1024)


def call(body, out_shape, operands, spaces, scratch=()):
    return pl.pallas_call(
        body,
        out_shape=out_shape,
        in_specs=list(spaces),
        out_specs=jax.tree.map(lambda _: VMEM, out_shape),
        scratch_shapes=list(scratch),
        compiler_params=PARAMS,
    )(*operands)


def shaped(rows, columns, dtype=BF16):
    return jax.ShapeDtypeStruct((rows, columns), dtype)


def swap(value, mask):
    return lax.ppermute(value, AXES, [(i, i ^ mask) for i in range(DEVICES)])


def over_quad(value):
    return [value] + [swap(value, 2 * q) for q in range(1, QUAD)]


def over_planes(value):
    second = swap(value, 16)
    return [value, swap(value, 8), second, swap(second, 8)]


def chip(pos):
    return (pos[0] >> 1) & 3


def lanes_of(column):
    return pl.ds(pl.multiple_of(column * LANES, LANES), LANES)


def pack_body(pos, *refs):
    tables, (features, cotangent, tiles, back_tiles) = refs[:4], refs[4:8]
    outs, tile_outs, scalars, sems = refs[8:12], refs[12:14], refs[14:18], refs[18]
    copies = [(table, scalar) for table, scalar in zip(tables, scalars)]
    for q, out in enumerate(outs):
        share = lanes_of(chip(pos) ^ q)
        copies.append((features.at[:, share], out.at[pl.ds(0, ROWS), pl.ds(0, LANES)]))
        copies.append((cotangent.at[:, share], out.at[pl.ds(0, ROWS), pl.ds(LANES, LANES)]))
    copies += [(tiles, tile_outs[0]), (back_tiles, tile_outs[1])]
    copies = [pltpu.make_async_copy(a, b, sems.at[i]) for i, (a, b) in enumerate(copies)]
    for copy in copies:
        copy.start()
    for copy in copies[:4]:
        copy.wait()
    line = lax.broadcasted_iota(jnp.int32, (16, LANES), 0)
    lane = lax.broadcasted_iota(jnp.int32, (16, LANES), 1)
    codes = jnp.full((16, LANES), -1, jnp.int32)
    for r in range(2):
        table, count = scalars[2 * r], scalars[2 * r + 1]
        for w in range(2):
            for s in range(SLOTS):
                value = jnp.where(s < count[w], table[w, s], -1)
                codes = jnp.where((line == 2 * r + w) & (lane == s), value, codes)
    codes = codes.astype(F32).astype(BF16)
    for out in outs:
        out[ROWS:, :LANES] = codes
        out[ROWS:, LANES:] = codes
    for copy in copies[4:]:
        copy.wait()


def pack(pos, *operands):
    operands = [pltpu.with_memory_space_constraint(operand, pltpu.HBM) for operand in operands]
    tile_shape = jax.ShapeDtypeStruct((2, BLOCK, SLOTS * BLOCK), BF16)
    return call(
        pack_body,
        (shaped(ROWS + 16, 2 * LANES),) * QUAD + (tile_shape,) * 2,
        (pos, *operands),
        [SMEM] + [HBM] * 8,
        [pltpu.SMEM((2, SLOTS), jnp.int32), pltpu.SMEM((2,), jnp.int32)] * 2
        + [pltpu.SemaphoreType.DMA((14,))],
    )


def unpack_body(pos, *refs):
    parts, (both, places) = refs[:QUAD], refs[QUAD:]
    for q, part in enumerate(parts):
        both[pl.ds(q * ROWS, ROWS), :] = part[:ROWS, :]
        block = part[ROWS:, :LANES].astype(F32).astype(jnp.int32)
        apart = (block >> 1) ^ pos[0]
        place = ((apart & 1) * 16 + (apart >> 3) * 4 + ((apart >> 1) & 3)) * 2 + (block & 1)
        place = jnp.where(block < 0, 2 * DEVICES, place)
        places[q * 8 : q * 8 + 8, :] = place[:8, :]


def unpack(pos, parts):
    return call(
        unpack_body,
        (shaped(SPAN, 2 * LANES), shaped(8 * QUAD, LANES, jnp.int32)),
        (pos, *parts),
        [SMEM] + [VMEM] * QUAD,
    )


def join_body(t0, t1, t2, t3, first, second):
    for i, tile in enumerate((t0, t1, t2, t3)):
        (first, second)[i // 2][pl.ds(2 * (i % 2), 2)] = tile[...]


def join(tiles):
    shape = jax.ShapeDtypeStruct((4, BLOCK, SLOTS * BLOCK), BF16)
    return call(join_body, (shape, shape), tiles, [VMEM] * 4)


X_THEN_Y, Y_THEN_X = (0, 1, 2, 3), (0, 2, 1, 3)


def mix_rows(base, half, order, places, shares, tiles, table, picked, store):
    for i, share in enumerate(shares):
        table[pl.ds(i * SPAN, SPAN), :] = share[:, pl.ds(half * LANES, LANES)]
    table[DEVICES * ROWS :, :] = jnp.zeros((BLOCK, LANES), BF16)
    for q in range(QUAD):
        for w in range(2):
            row = q * 2 + w
            for s in range(SLOTS):
                first = pl.multiple_of(places[q * 8 + base + w, s] * BLOCK, BLOCK)
                picked[row, pl.ds(s * BLOCK, BLOCK), :] = table[pl.ds(first, BLOCK), :]
            tile = tiles[order[q] // 2][2 * (order[q] % 2) + w]
            total = jnp.dot(tile, picked[row], preferred_element_type=F32)
            total = total + table[pl.ds(row * BLOCK, BLOCK), :].astype(F32)
            store(q, w, total.astype(BF16))


MIX_SCRATCH = (
    pltpu.VMEM((DEVICES * ROWS + BLOCK, LANES), BF16),
    pltpu.VMEM((2 * QUAD, SLOTS * BLOCK, LANES), BF16),
)


def mix_body(base, half, order, places, *refs):
    shares, tiles, (out, table, picked) = refs[:8], refs[8:10], refs[10:]

    def store(q, w, rows):
        out[pl.ds(q * ROWS + w * BLOCK, BLOCK), :] = rows

    mix_rows(base, half, order, places, shares, tiles, table, picked, store)


def mix(places, base, half, order, shares, tiles):
    return call(
        functools.partial(mix_body, base, half, order),
        shaped(SPAN, LANES),
        (places, *shares, *tiles),
        [SMEM] + [VMEM] * 10,
        MIX_SCRATCH,
    )


def mix_beside_body(places, *refs):
    shares, tiles, total = refs[:8], refs[8:10], refs[10]
    outs, (table, picked) = refs[11:15], refs[15:]
    extent = total.shape[0]
    for out in outs:
        out[:extent, :] = total[...]

    def store(q, w, rows):
        outs[q][pl.ds(extent + w * BLOCK, BLOCK), :] = rows

    mix_rows(0, 0, X_THEN_Y, places, shares, tiles, table, picked, store)


def mix_beside(places, shares, tiles, total):
    return call(
        mix_beside_body,
        (shaped(total.shape[0] + ROWS, LANES),) * QUAD,
        (places, *shares, *tiles, total),
        [SMEM] + [VMEM] * 11,
        MIX_SCRATCH,
    )


def whole_rows(pos, pieces, target):
    for p, piece in enumerate(pieces):
        share = lanes_of(chip(pos) ^ p)
        for q in range(QUAD):
            target[pl.ds(q * ROWS, ROWS), share] = piece[pl.ds((p ^ q) * ROWS, ROWS), :]


def first_body(pos, p0, p1, p2, p3, w_first, mixed, hidden, hidden_share, slope, full):
    whole_rows(pos, (p0, p1, p2, p3), mixed)
    pre = jnp.dot(mixed[...], w_first[...], preferred_element_type=F32)
    sig = jax.nn.sigmoid(pre)
    hidden[...] = (pre * sig).astype(BF16)
    full[...] = sig * (1.0 + pre * (1.0 - sig))
    share = lanes_of(chip(pos))
    hidden_share[...] = hidden[:, share]
    slope[...] = full[:, share]


def first_layer(pos, pieces, w_first):
    channels = w_first.shape[0]
    return call(
        first_body,
        (
            shaped(SPAN, channels),
            shaped(SPAN, channels),
            shaped(SPAN, LANES),
            shaped(SPAN, LANES, F32),
        ),
        (pos, *pieces, w_first),
        [SMEM] + [VMEM] * 5,
        [pltpu.VMEM((SPAN, channels), F32)],
    )


def second_body(pos, p0, p1, p2, p3, w_second, z_out):
    total = jnp.zeros(z_out.shape, F32)
    for p, piece in enumerate((p0, p1, p2, p3)):
        total = total + jnp.dot(
            piece[piece.shape[0] - ROWS :, :],
            w_second[lanes_of(chip(pos) ^ p), :],
            preferred_element_type=F32,
        )
    z_out[...] = total.astype(BF16)


def second_layer(pos, pieces, w_second):
    return call(
        second_body,
        shaped(ROWS, w_second.shape[0]),
        (pos, *pieces, w_second),
        [SMEM] + [VMEM] * 5,
    )


def grads_body(pos, mixed, hidden, slope, p0, p1, p2, p3, w_second, keep, send, spread):
    whole_rows(pos, (p0, p1, p2, p3), spread)
    back_hidden = lax.dot_general(
        spread[...],
        w_second[lanes_of(chip(pos)), :],
        (((1,), (1,)), ((), ())),
        preferred_element_type=F32,
    )
    back_first = (back_hidden * slope[...]).astype(BF16)
    over_rows = (((0,), (0,)), ((), ()))
    first = lax.dot_general(mixed[...], back_first, over_rows, preferred_element_type=F32)
    second = lax.dot_general(hidden[...], p0[...], over_rows, preferred_element_type=F32)
    keeps_first = (pos[0] & 1) == 0

    @pl.when(keeps_first)
    def _():
        keep[...] = first
        send[...] = second

    @pl.when(jnp.logical_not(keeps_first))
    def _():
        keep[...] = second
        send[...] = first


def gradients(pos, mixed, hidden, slope, pieces, w_second):
    channels = w_second.shape[0]
    return call(
        grads_body,
        (shaped(channels, LANES, F32), shaped(channels, LANES, F32)),
        (pos, mixed, hidden, slope, *pieces, w_second),
        [SMEM] + [VMEM] * 8,
        [pltpu.VMEM((SPAN, channels), BF16)],
    )


def place_body(pos, *refs):
    mine, other, (first, second) = refs[:QUAD], refs[QUAD : 2 * QUAD], refs[2 * QUAD :]
    extent = first.shape[0]
    keeps_first = (pos[0] & 1) == 0

    def fill(mine_out, other_out):
        for p in range(QUAD):
            share = lanes_of(chip(pos) ^ p)
            mine_out[:, share] = mine[p][:extent, :].astype(F32)
            other_out[:, share] = other[p][:extent, :].astype(F32)

    @pl.when(keeps_first)
    def _():
        fill(first, second)

    @pl.when(jnp.logical_not(keeps_first))
    def _():
        fill(second, first)


def place(pos, mine, other):
    channels = QUAD * LANES
    return call(
        place_body,
        (shaped(channels, channels, F32),) * 2,
        (pos, *mine, *other),
        [SMEM] + [VMEM] * (2 * QUAD),
    )


def planned_shards(
    features,
    tile_entries,
    tile_columns,
    tiles_per_row,
    rev_vals,
    rev_cols,
    rev_count,
    w_first,
    w_second,
    cotangent,
):
    pos = lax.axis_index(AXES).astype(jnp.int32).reshape(1)
    *packed, tiles, back_tiles = pack(
        pos,
        tile_columns,
        tiles_per_row,
        rev_cols,
        rev_count,
        features,
        cotangent,
        tile_entries,
        rev_vals,
    )
    parts = [packed[0]] + [swap(packed[q], 2 * q) for q in range(1, QUAD)]
    share, places = unpack(pos, parts)
    tiles, back_tiles = join((tiles, swap(tiles, 2), back_tiles, swap(back_tiles, 4)))
    tiles = (tiles, swap(tiles, 4))
    back_tiles = (back_tiles, swap(back_tiles, 2))

    def everywhere(own):
        planes = over_planes(own)
        return planes + [swap(plane, CORE) for plane in planes]

    shares = everywhere(share)
    mixed_share = mix(places, 0, 0, X_THEN_Y, shares, tiles)
    spread_share = mix(places, 2, 1, Y_THEN_X, shares, back_tiles)
    mixed, hidden, hidden_share, slope = first_layer(pos, over_quad(mixed_share), w_first)
    by_one, by_two = swap(hidden_share, 8), swap(hidden_share, 16)
    keep, send = gradients(pos, mixed, hidden, slope, over_quad(spread_share), w_second)
    total = (keep + swap(send, CORE)).astype(BF16)
    across = swap(total, 8)
    total = (total.astype(F32) + across.astype(F32)).astype(BF16)
    by_two, _ = lax.optimization_barrier((by_two, across))
    planes = [hidden_share, by_one, by_two, swap(by_two, 8)]
    total = (total.astype(F32) + swap(total, 16).astype(F32)).astype(BF16)
    planes += [swap(plane, CORE) for plane in planes]
    beside = mix_beside(places, planes, tiles, total)
    mine = [beside[0]] + [swap(beside[q], 2 * q) for q in range(1, QUAD)]
    z_out = second_layer(pos, mine, w_second)
    grad_first, grad_second = place(pos, mine, [swap(piece, CORE) for piece in mine])
    return (z_out, grad_first, grad_second)


def solution(mesh):
    placed = (
        P(AXES, None),
        P(AXES, None, None),
        P(AXES, None),
        P(AXES),
        P(AXES, None, None),
        P(AXES, None),
        P(AXES),
        P(),
        P(),
        P(AXES, None),
    )
    planned = mesh.shape["rows"] == 8 and mesh.shape["grp"] == 4
    return jax.shard_map(
        planned_shards if planned else gathered_shards,
        mesh=mesh,
        in_specs=placed,
        out_specs=(P(AXES, None), P(), P()),
        check_vma=False,
    )
```

```python
import functools

import jax
import jax.numpy as jnp
from jax import lax
from jax.experimental import pallas as pl
from jax.experimental.pallas import tpu as pltpu
from jax.sharding import PartitionSpec as P

AXES = ("rows", "grp")
F32 = jnp.float32
BF16 = jnp.bfloat16


def aggregate(panel_vals, strip_columns, strip_count, everyone, own_rows):
    blocks, size_block, span_width = panel_vals.shape
    slot_count = span_width // size_block
    channels = everyone.shape[1]
    block_table = everyone.reshape(-1, size_block, channels)
    slot_ids = lax.broadcasted_iota(jnp.int32, strip_columns.shape, 1)
    weights = (slot_ids < strip_count[:, None]).astype(everyone.dtype)
    picked = (block_table[strip_columns] * weights[:, :, None, None]).reshape(
        blocks, slot_count * size_block, channels
    )
    summed_rows = jnp.einsum("bik,bkc->bic", panel_vals, picked, preferred_element_type=F32)
    return summed_rows.reshape(blocks * size_block, channels) + own_rows.astype(F32)


def gathered_shards(
    features,
    tile_entries,
    tile_columns,
    tiles_per_row,
    rev_vals,
    rev_cols,
    rev_count,
    w_first,
    w_second,
    cotangent,
):
    channels = features.shape[1]
    pair = jnp.concatenate([features, cotangent], axis=1)
    pair_all = lax.all_gather(pair, AXES, axis=0, tiled=True)
    mixed_own = aggregate(
        tile_entries, tile_columns, tiles_per_row, pair_all[:, :channels], features
    ).astype(BF16)
    spread_own = aggregate(
        rev_vals, rev_cols, rev_count, pair_all[:, channels:], cotangent
    ).astype(BF16)
    both_all = lax.all_gather(
        jnp.concatenate([mixed_own, spread_own], axis=1), AXES, axis=0, tiled=True
    )
    mixed = both_all[:, :channels]
    spread = both_all[:, channels:]
    pre_first = jnp.dot(mixed, w_first, preferred_element_type=F32)
    sig = jax.nn.sigmoid(pre_first)
    hidden = (pre_first * sig).astype(BF16)
    slope = sig * (1.0 + pre_first * (1.0 - sig))
    back_hidden = lax.dot_general(
        spread, w_second, (((1,), (1,)), ((), ())), preferred_element_type=F32
    )
    back_first = (back_hidden * slope).astype(BF16)
    grad_first = lax.dot_general(
        mixed, back_first, (((0,), (0,)), ((), ())), preferred_element_type=F32
    )
    grad_second = lax.dot_general(
        hidden, spread, (((0,), (0,)), ((), ())), preferred_element_type=F32
    )
    position = lax.axis_index(AXES) * features.shape[0]
    hidden_own = lax.dynamic_slice_in_dim(hidden, position, features.shape[0], 0)
    mixed_second = aggregate(
        tile_entries, tile_columns, tiles_per_row, hidden, hidden_own
    ).astype(BF16)
    z_out = jnp.dot(mixed_second, w_second, preferred_element_type=F32).astype(BF16)
    return (z_out, grad_first, grad_second)


CORE = 1
DEVICES, QUAD, PLANES, SLOTS, BLOCK = 32, 4, 4, 16, 64
GROUP = 8
LANES = 128
ROWS = 128
SPAN = QUAD * ROWS
VMEM = pl.BlockSpec(memory_space=pltpu.VMEM)
SMEM = pl.BlockSpec(memory_space=pltpu.SMEM)
HBM = pl.BlockSpec(memory_space=pltpu.HBM)
PARAMS = pltpu.CompilerParams(vmem_limit_bytes=48 * 1024 * 1024)


def call(body, out_shape, operands, spaces, scratch=()):
    return pl.pallas_call(
        body,
        out_shape=out_shape,
        in_specs=list(spaces),
        out_specs=jax.tree.map(lambda _: VMEM, out_shape),
        scratch_shapes=list(scratch),
        compiler_params=PARAMS,
    )(*operands)


def shaped(rows, columns, dtype=BF16):
    return jax.ShapeDtypeStruct((rows, columns), dtype)


def swap(value, mask):
    return lax.ppermute(value, AXES, [(i, i ^ mask) for i in range(DEVICES)])


def over_quad(value):
    return [value] + [swap(value, 2 * q) for q in range(1, QUAD)]


def over_planes(value):
    second = swap(value, 16)
    return [value, swap(value, 8), second, swap(second, 8)]


def chip(pos):
    return (pos[0] >> 1) & 3


def lanes_of(column):
    return pl.ds(pl.multiple_of(column * LANES, LANES), LANES)


def pack_body(pos, *refs):
    tables, (features, cotangent, tiles, back_tiles) = refs[:4], refs[4:8]
    outs, tile_outs, scalars, sems = refs[8:12], refs[12:14], refs[14:18], refs[18]
    copies = [(table, scalar) for table, scalar in zip(tables, scalars)]
    for q, out in enumerate(outs):
        share = lanes_of(chip(pos) ^ q)
        copies.append((features.at[:, share], out.at[pl.ds(0, ROWS), pl.ds(0, LANES)]))
        copies.append((cotangent.at[:, share], out.at[pl.ds(0, ROWS), pl.ds(LANES, LANES)]))
    copies += [(tiles, tile_outs[0]), (back_tiles, tile_outs[1])]
    copies = [pltpu.make_async_copy(a, b, sems.at[i]) for i, (a, b) in enumerate(copies)]
    for copy in copies:
        copy.start()
    for copy in copies[:4]:
        copy.wait()
    line = lax.broadcasted_iota(jnp.int32, (16, LANES), 0)
    lane = lax.broadcasted_iota(jnp.int32, (16, LANES), 1)
    codes = jnp.full((16, LANES), -1, jnp.int32)
    for r in range(2):
        table, count = scalars[2 * r], scalars[2 * r + 1]
        for w in range(2):
            for s in range(SLOTS):
                value = jnp.where(s < count[w], table[w, s], -1)
                codes = jnp.where((line == 2 * r + w) & (lane == s), value, codes)
    codes = codes.astype(F32).astype(BF16)
    for out in outs:
        out[ROWS:, :LANES] = codes
        out[ROWS:, LANES:] = codes
    for copy in copies[4:]:
        copy.wait()


def pack(pos, *operands):
    operands = [pltpu.with_memory_space_constraint(operand, pltpu.HBM) for operand in operands]
    tile_shape = jax.ShapeDtypeStruct((2, BLOCK, SLOTS * BLOCK), BF16)
    return call(
        pack_body,
        (shaped(ROWS + 16, 2 * LANES),) * QUAD + (tile_shape,) * 2,
        (pos, *operands),
        [SMEM] + [HBM] * 8,
        [pltpu.SMEM((2, SLOTS), jnp.int32), pltpu.SMEM((2,), jnp.int32)] * 2
        + [pltpu.SemaphoreType.DMA((14,))],
    )


def unpack_body(pos, *refs):
    parts, (both, places) = refs[:QUAD], refs[QUAD:]
    for q, part in enumerate(parts):
        both[pl.ds(q * ROWS, ROWS), :] = part[:ROWS, :]
        block = part[ROWS:, :LANES].astype(F32).astype(jnp.int32)
        apart = (block >> 1) ^ pos[0]
        place = ((apart & 1) * 16 + (apart >> 3) * 4 + ((apart >> 1) & 3)) * 2 + (block & 1)
        place = jnp.where(block < 0, 2 * DEVICES, place)
        places[q * 8 : q * 8 + 8, :] = place[:8, :]


def unpack(pos, parts):
    return call(
        unpack_body,
        (shaped(SPAN, 2 * LANES), shaped(8 * QUAD, LANES, jnp.int32)),
        (pos, *parts),
        [SMEM] + [VMEM] * QUAD,
    )


def join_body(t0, t1, t2, t3, first, second):
    for i, tile in enumerate((t0, t1, t2, t3)):
        (first, second)[i // 2][pl.ds(2 * (i % 2), 2)] = tile[...]


def join(tiles):
    shape = jax.ShapeDtypeStruct((4, BLOCK, SLOTS * BLOCK), BF16)
    return call(join_body, (shape, shape), tiles, [VMEM] * 4)


X_THEN_Y, Y_THEN_X = (0, 1, 2, 3), (0, 2, 1, 3)


def mix_rows(base, half, order, places, shares, tiles, table, store):
    for i, share in enumerate(shares):
        table[pl.ds(i * SPAN, SPAN), :] = share[:, pl.ds(half * LANES, LANES)]
    table[DEVICES * ROWS :, :] = jnp.zeros((BLOCK, LANES), BF16)
    for q in range(QUAD):
        for w in range(2):
            row = q * 2 + w
            tile = tiles[order[q] // 2].at[2 * (order[q] % 2) + w]
            total = table[pl.ds(row * BLOCK, BLOCK), :].astype(F32)
            for start in range(0, SLOTS, GROUP):
                blocks = []
                for s in range(start, start + GROUP):
                    first = pl.multiple_of(places[q * 8 + base + w, s] * BLOCK, BLOCK)
                    blocks.append(table[pl.ds(first, BLOCK), :])
                total = total + jnp.dot(
                    tile[:, pl.ds(start * BLOCK, GROUP * BLOCK)],
                    jnp.concatenate(blocks, axis=0),
                    preferred_element_type=F32,
                )
            store(q, w, total.astype(BF16))


MIX_SCRATCH = (pltpu.VMEM((DEVICES * ROWS + BLOCK, LANES), BF16),)


def mix_body(base, half, order, places, *refs):
    shares, tiles, (out, table) = refs[:8], refs[8:10], refs[10:]

    def store(q, w, rows):
        out[pl.ds(q * ROWS + w * BLOCK, BLOCK), :] = rows

    mix_rows(base, half, order, places, shares, tiles, table, store)


def mix(places, base, half, order, shares, tiles):
    return call(
        functools.partial(mix_body, base, half, order),
        shaped(SPAN, LANES),
        (places, *shares, *tiles),
        [SMEM] + [VMEM] * 10,
        MIX_SCRATCH,
    )


def mix_beside_body(places, *refs):
    shares, tiles, total = refs[:8], refs[8:10], refs[10]
    outs, table = refs[11:15], refs[15]
    extent = total.shape[0]
    for out in outs:
        out[:extent, :] = total[...]

    def store(q, w, rows):
        outs[q][pl.ds(extent + w * BLOCK, BLOCK), :] = rows

    mix_rows(0, 0, X_THEN_Y, places, shares, tiles, table, store)


def mix_beside(places, shares, tiles, total):
    return call(
        mix_beside_body,
        (shaped(total.shape[0] + ROWS, LANES),) * QUAD,
        (places, *shares, *tiles, total),
        [SMEM] + [VMEM] * 11,
        MIX_SCRATCH,
    )


def whole_rows(pos, pieces, target):
    for p, piece in enumerate(pieces):
        share = lanes_of(chip(pos) ^ p)
        for q in range(QUAD):
            target[pl.ds(q * ROWS, ROWS), share] = piece[pl.ds((p ^ q) * ROWS, ROWS), :]


def first_body(pos, p0, p1, p2, p3, w_first, mixed, hidden, hidden_share, slope, full):
    whole_rows(pos, (p0, p1, p2, p3), mixed)
    pre = jnp.dot(mixed[...], w_first[...], preferred_element_type=F32)
    sig = jax.nn.sigmoid(pre)
    hidden[...] = (pre * sig).astype(BF16)
    full[...] = sig * (1.0 + pre * (1.0 - sig))
    share = lanes_of(chip(pos))
    hidden_share[...] = hidden[:, share]
    slope[...] = full[:, share]


def first_layer(pos, pieces, w_first):
    channels = w_first.shape[0]
    return call(
        first_body,
        (
            shaped(SPAN, channels),
            shaped(SPAN, channels),
            shaped(SPAN, LANES),
            shaped(SPAN, LANES, F32),
        ),
        (pos, *pieces, w_first),
        [SMEM] + [VMEM] * 5,
        [pltpu.VMEM((SPAN, channels), F32)],
    )


def second_body(pos, p0, p1, p2, p3, w_second, z_out):
    total = jnp.zeros(z_out.shape, F32)
    for p, piece in enumerate((p0, p1, p2, p3)):
        total = total + jnp.dot(
            piece[piece.shape[0] - ROWS :, :],
            w_second[lanes_of(chip(pos) ^ p), :],
            preferred_element_type=F32,
        )
    z_out[...] = total.astype(BF16)


def second_layer(pos, pieces, w_second):
    return call(
        second_body,
        shaped(ROWS, w_second.shape[0]),
        (pos, *pieces, w_second),
        [SMEM] + [VMEM] * 5,
    )


def grads_body(pos, mixed, hidden, slope, p0, p1, p2, p3, w_second, keep, send, spread):
    whole_rows(pos, (p0, p1, p2, p3), spread)
    back_hidden = lax.dot_general(
        spread[...],
        w_second[lanes_of(chip(pos)), :],
        (((1,), (1,)), ((), ())),
        preferred_element_type=F32,
    )
    back_first = (back_hidden * slope[...]).astype(BF16)
    over_rows = (((0,), (0,)), ((), ()))
    first = lax.dot_general(mixed[...], back_first, over_rows, preferred_element_type=F32)
    second = lax.dot_general(hidden[...], p0[...], over_rows, preferred_element_type=F32)
    keeps_first = (pos[0] & 1) == 0

    @pl.when(keeps_first)
    def _():
        keep[...] = first
        send[...] = second

    @pl.when(jnp.logical_not(keeps_first))
    def _():
        keep[...] = second
        send[...] = first


def gradients(pos, mixed, hidden, slope, pieces, w_second):
    channels = w_second.shape[0]
    return call(
        grads_body,
        (shaped(channels, LANES, F32), shaped(channels, LANES, F32)),
        (pos, mixed, hidden, slope, *pieces, w_second),
        [SMEM] + [VMEM] * 8,
        [pltpu.VMEM((SPAN, channels), BF16)],
    )


def place_body(pos, *refs):
    mine, other, (first, second) = refs[:QUAD], refs[QUAD : 2 * QUAD], refs[2 * QUAD :]
    extent = first.shape[0]
    keeps_first = (pos[0] & 1) == 0

    def fill(mine_out, other_out):
        for p in range(QUAD):
            share = lanes_of(chip(pos) ^ p)
            mine_out[:, share] = mine[p][:extent, :].astype(F32)
            other_out[:, share] = other[p][:extent, :].astype(F32)

    @pl.when(keeps_first)
    def _():
        fill(first, second)

    @pl.when(jnp.logical_not(keeps_first))
    def _():
        fill(second, first)


def place(pos, mine, other):
    channels = QUAD * LANES
    return call(
        place_body,
        (shaped(channels, channels, F32),) * 2,
        (pos, *mine, *other),
        [SMEM] + [VMEM] * (2 * QUAD),
    )


def planned_shards(
    features,
    tile_entries,
    tile_columns,
    tiles_per_row,
    rev_vals,
    rev_cols,
    rev_count,
    w_first,
    w_second,
    cotangent,
):
    pos = lax.axis_index(AXES).astype(jnp.int32).reshape(1)
    *packed, tiles, back_tiles = pack(
        pos,
        tile_columns,
        tiles_per_row,
        rev_cols,
        rev_count,
        features,
        cotangent,
        tile_entries,
        rev_vals,
    )
    parts = [packed[0]] + [swap(packed[q], 2 * q) for q in range(1, QUAD)]
    share, places = unpack(pos, parts)
    tiles, back_tiles = join((tiles, swap(tiles, 2), back_tiles, swap(back_tiles, 4)))
    tiles = (tiles, swap(tiles, 4))
    back_tiles = (back_tiles, swap(back_tiles, 2))

    def everywhere(own):
        planes = over_planes(own)
        return planes + [swap(plane, CORE) for plane in planes]

    shares = everywhere(share)
    mixed_share = mix(places, 0, 0, X_THEN_Y, shares, tiles)
    spread_share = mix(places, 2, 1, Y_THEN_X, shares, back_tiles)
    mixed, hidden, hidden_share, slope = first_layer(pos, over_quad(mixed_share), w_first)
    by_one, by_two = swap(hidden_share, 8), swap(hidden_share, 16)
    keep, send = gradients(pos, mixed, hidden, slope, over_quad(spread_share), w_second)
    total = (keep + swap(send, CORE)).astype(BF16)
    across = swap(total, 8)
    total = (total.astype(F32) + across.astype(F32)).astype(BF16)
    by_two, _ = lax.optimization_barrier((by_two, across))
    planes = [hidden_share, by_one, by_two, swap(by_two, 8)]
    total = (total.astype(F32) + swap(total, 16).astype(F32)).astype(BF16)
    planes += [swap(plane, CORE) for plane in planes]
    beside = mix_beside(places, planes, tiles, total)
    mine = [beside[0]] + [swap(beside[q], 2 * q) for q in (3, 2, 1)][::-1]
    z_out = second_layer(pos, mine, w_second)
    grad_first, grad_second = place(pos, mine, [swap(piece, CORE) for piece in mine])
    return (z_out, grad_first, grad_second)


def solution(mesh):
    placed = (
        P(AXES, None),
        P(AXES, None, None),
        P(AXES, None),
        P(AXES),
        P(AXES, None, None),
        P(AXES, None),
        P(AXES),
        P(),
        P(),
        P(AXES, None),
    )
    planned = mesh.shape["rows"] == 8 and mesh.shape["grp"] == 4
    return jax.shard_map(
        planned_shards if planned else gathered_shards,
        mesh=mesh,
        in_specs=placed,
        out_specs=(P(AXES, None), P(), P()),
        check_vma=False,
    )
```

```python
import functools

import jax
import jax.numpy as jnp
from jax import lax
from jax.experimental import pallas as pl
from jax.experimental.pallas import tpu as pltpu
from jax.sharding import PartitionSpec as P

AXES = ("rows", "grp")
F32 = jnp.float32
BF16 = jnp.bfloat16


def aggregate(panel_vals, strip_columns, strip_count, everyone, own_rows):
    blocks, size_block, span_width = panel_vals.shape
    slot_count = span_width // size_block
    channels = everyone.shape[1]
    block_table = everyone.reshape(-1, size_block, channels)
    slot_ids = lax.broadcasted_iota(jnp.int32, strip_columns.shape, 1)
    weights = (slot_ids < strip_count[:, None]).astype(everyone.dtype)
    picked = (block_table[strip_columns] * weights[:, :, None, None]).reshape(
        blocks, slot_count * size_block, channels
    )
    summed_rows = jnp.einsum("bik,bkc->bic", panel_vals, picked, preferred_element_type=F32)
    return summed_rows.reshape(blocks * size_block, channels) + own_rows.astype(F32)


def gathered_shards(
    features,
    tile_entries,
    tile_columns,
    tiles_per_row,
    rev_vals,
    rev_cols,
    rev_count,
    w_first,
    w_second,
    cotangent,
):
    channels = features.shape[1]
    pair = jnp.concatenate([features, cotangent], axis=1)
    pair_all = lax.all_gather(pair, AXES, axis=0, tiled=True)
    mixed_own = aggregate(
        tile_entries, tile_columns, tiles_per_row, pair_all[:, :channels], features
    ).astype(BF16)
    spread_own = aggregate(
        rev_vals, rev_cols, rev_count, pair_all[:, channels:], cotangent
    ).astype(BF16)
    both_all = lax.all_gather(
        jnp.concatenate([mixed_own, spread_own], axis=1), AXES, axis=0, tiled=True
    )
    mixed = both_all[:, :channels]
    spread = both_all[:, channels:]
    pre_first = jnp.dot(mixed, w_first, preferred_element_type=F32)
    sig = jax.nn.sigmoid(pre_first)
    hidden = (pre_first * sig).astype(BF16)
    slope = sig * (1.0 + pre_first * (1.0 - sig))
    back_hidden = lax.dot_general(
        spread, w_second, (((1,), (1,)), ((), ())), preferred_element_type=F32
    )
    back_first = (back_hidden * slope).astype(BF16)
    grad_first = lax.dot_general(
        mixed, back_first, (((0,), (0,)), ((), ())), preferred_element_type=F32
    )
    grad_second = lax.dot_general(
        hidden, spread, (((0,), (0,)), ((), ())), preferred_element_type=F32
    )
    position = lax.axis_index(AXES) * features.shape[0]
    hidden_own = lax.dynamic_slice_in_dim(hidden, position, features.shape[0], 0)
    mixed_second = aggregate(
        tile_entries, tile_columns, tiles_per_row, hidden, hidden_own
    ).astype(BF16)
    z_out = jnp.dot(mixed_second, w_second, preferred_element_type=F32).astype(BF16)
    return (z_out, grad_first, grad_second)


CORE = 1
DEVICES, QUAD, PLANES, SLOTS, BLOCK = 32, 4, 4, 16, 64
GROUP = 8
LANES = 128
ROWS = 128
SPAN = QUAD * ROWS
VMEM = pl.BlockSpec(memory_space=pltpu.VMEM)
SMEM = pl.BlockSpec(memory_space=pltpu.SMEM)
HBM = pl.BlockSpec(memory_space=pltpu.HBM)
PARAMS = pltpu.CompilerParams(vmem_limit_bytes=48 * 1024 * 1024)


def call(body, out_shape, operands, spaces, scratch=()):
    return pl.pallas_call(
        body,
        out_shape=out_shape,
        in_specs=list(spaces),
        out_specs=jax.tree.map(lambda _: VMEM, out_shape),
        scratch_shapes=list(scratch),
        compiler_params=PARAMS,
    )(*operands)


def shaped(rows, columns, dtype=BF16):
    return jax.ShapeDtypeStruct((rows, columns), dtype)


def swap(value, mask):
    return lax.ppermute(value, AXES, [(i, i ^ mask) for i in range(DEVICES)])


def over_quad(value):
    return [value] + [swap(value, 2 * q) for q in range(1, QUAD)]


def over_planes(value):
    second = swap(value, 16)
    return [value, swap(value, 8), second, swap(second, 8)]


def chip(pos):
    return (pos[0] >> 1) & 3


def lanes_of(column):
    return pl.ds(pl.multiple_of(column * LANES, LANES), LANES)


def pack_body(pos, *refs):
    tables, (features, cotangent, tiles, back_tiles) = refs[:4], refs[4:8]
    outs, tile_outs, scalars, sems = refs[8:12], refs[12:14], refs[14:18], refs[18]
    copies = [(table, scalar) for table, scalar in zip(tables, scalars)]
    for q, out in enumerate(outs):
        share = lanes_of(chip(pos) ^ q)
        copies.append((features.at[:, share], out.at[pl.ds(0, ROWS), pl.ds(0, LANES)]))
        copies.append((cotangent.at[:, share], out.at[pl.ds(0, ROWS), pl.ds(LANES, LANES)]))
    copies += [(tiles, tile_outs[0]), (back_tiles, tile_outs[1])]
    copies = [pltpu.make_async_copy(a, b, sems.at[i]) for i, (a, b) in enumerate(copies)]
    for copy in copies:
        copy.start()
    for copy in copies[:4]:
        copy.wait()
    line = lax.broadcasted_iota(jnp.int32, (16, LANES), 0)
    lane = lax.broadcasted_iota(jnp.int32, (16, LANES), 1)
    codes = jnp.full((16, LANES), -1, jnp.int32)
    for r in range(2):
        table, count = scalars[2 * r], scalars[2 * r + 1]
        for w in range(2):
            for s in range(SLOTS):
                value = jnp.where(s < count[w], table[w, s], -1)
                codes = jnp.where((line == 2 * r + w) & (lane == s), value, codes)
    codes = codes.astype(F32).astype(BF16)
    for out in outs:
        out[ROWS:, :LANES] = codes
        out[ROWS:, LANES:] = codes
    for copy in copies[4:]:
        copy.wait()


def pack(pos, *operands):
    operands = [pltpu.with_memory_space_constraint(operand, pltpu.HBM) for operand in operands]
    tile_shape = jax.ShapeDtypeStruct((2, BLOCK, SLOTS * BLOCK), BF16)
    return call(
        pack_body,
        (shaped(ROWS + 16, 2 * LANES),) * QUAD + (tile_shape,) * 2,
        (pos, *operands),
        [SMEM] + [HBM] * 8,
        [pltpu.SMEM((2, SLOTS), jnp.int32), pltpu.SMEM((2,), jnp.int32)] * 2
        + [pltpu.SemaphoreType.DMA((14,))],
    )


def unpack_body(pos, *refs):
    parts, (both, places) = refs[:QUAD], refs[QUAD:]
    for q, part in enumerate(parts):
        both[pl.ds(q * ROWS, ROWS), :] = part[:ROWS, :]
        block = part[ROWS:, :LANES].astype(F32).astype(jnp.int32)
        apart = (block >> 1) ^ pos[0]
        place = ((apart & 1) * 16 + (apart >> 3) * 4 + ((apart >> 1) & 3)) * 2 + (block & 1)
        place = jnp.where(block < 0, 2 * DEVICES, place)
        places[q * 8 : q * 8 + 8, :] = place[:8, :]


def unpack(pos, parts):
    return call(
        unpack_body,
        (shaped(SPAN, 2 * LANES), shaped(8 * QUAD, LANES, jnp.int32)),
        (pos, *parts),
        [SMEM] + [VMEM] * QUAD,
    )


def join_body(t0, t1, t2, t3, first, second):
    for i, tile in enumerate((t0, t1, t2, t3)):
        (first, second)[i // 2][pl.ds(2 * (i % 2), 2)] = tile[...]


def join(tiles):
    shape = jax.ShapeDtypeStruct((4, BLOCK, SLOTS * BLOCK), BF16)
    return call(join_body, (shape, shape), tiles, [VMEM] * 4)


X_THEN_Y, Y_THEN_X = (0, 1, 2, 3), (0, 2, 1, 3)


def mix_rows(base, half, order, places, shares, tiles, table, store):
    for i, share in enumerate(shares):
        table[pl.ds(i * SPAN, SPAN), :] = share[:, pl.ds(half * LANES, LANES)]
    table[DEVICES * ROWS :, :] = jnp.zeros((BLOCK, LANES), BF16)
    for q in range(QUAD):
        for w in range(2):
            row = q * 2 + w
            tile = tiles[order[q] // 2].at[2 * (order[q] % 2) + w]
            total = table[pl.ds(row * BLOCK, BLOCK), :].astype(F32)
            for start in range(0, SLOTS, GROUP):
                blocks = []
                for s in range(start, start + GROUP):
                    first = pl.multiple_of(places[q * 8 + base + w, s] * BLOCK, BLOCK)
                    blocks.append(table[pl.ds(first, BLOCK), :])
                total = total + jnp.dot(
                    tile[:, pl.ds(start * BLOCK, GROUP * BLOCK)],
                    jnp.concatenate(blocks, axis=0),
                    preferred_element_type=F32,
                )
            store(q, w, total.astype(BF16))


MIX_SCRATCH = (pltpu.VMEM((DEVICES * ROWS + BLOCK, LANES), BF16),)


def mix_body(base, half, order, places, *refs):
    shares, tiles, (out, table) = refs[:8], refs[8:10], refs[10:]

    def store(q, w, rows):
        out[pl.ds(q * ROWS + w * BLOCK, BLOCK), :] = rows

    mix_rows(base, half, order, places, shares, tiles, table, store)


def mix(places, base, half, order, shares, tiles):
    return call(
        functools.partial(mix_body, base, half, order),
        shaped(SPAN, LANES),
        (places, *shares, *tiles),
        [SMEM] + [VMEM] * 10,
        MIX_SCRATCH,
    )


def mix_beside_body(places, *refs):
    shares, tiles, total = refs[:8], refs[8:10], refs[10]
    outs, table = refs[11:15], refs[15]
    extent = total.shape[0]
    for out in outs:
        out[:extent, :] = total[...]

    def store(q, w, rows):
        outs[q][pl.ds(extent + w * BLOCK, BLOCK), :] = rows

    mix_rows(0, 0, X_THEN_Y, places, shares, tiles, table, store)


def mix_beside(places, shares, tiles, total):
    return call(
        mix_beside_body,
        (shaped(total.shape[0] + ROWS, LANES),) * QUAD,
        (places, *shares, *tiles, total),
        [SMEM] + [VMEM] * 11,
        MIX_SCRATCH,
    )


def whole_rows(pos, pieces, target):
    for p, piece in enumerate(pieces):
        share = lanes_of(chip(pos) ^ p)
        for q in range(QUAD):
            target[pl.ds(q * ROWS, ROWS), share] = piece[pl.ds((p ^ q) * ROWS, ROWS), :]


def first_body(pos, p0, p1, p2, p3, w_first, mixed, hidden, hidden_share, slope, full):
    whole_rows(pos, (p0, p1, p2, p3), mixed)
    pre = jnp.dot(mixed[...], w_first[...], preferred_element_type=F32)
    sig = jax.nn.sigmoid(pre)
    hidden[...] = (pre * sig).astype(BF16)
    full[...] = sig * (1.0 + pre * (1.0 - sig))
    share = lanes_of(chip(pos))
    hidden_share[...] = hidden[:, share]
    slope[...] = full[:, share]


def first_layer(pos, pieces, w_first):
    channels = w_first.shape[0]
    return call(
        first_body,
        (
            shaped(SPAN, channels),
            shaped(SPAN, channels),
            shaped(SPAN, LANES),
            shaped(SPAN, LANES, F32),
        ),
        (pos, *pieces, w_first),
        [SMEM] + [VMEM] * 5,
        [pltpu.VMEM((SPAN, channels), F32)],
    )


def second_body(pos, p0, p1, p2, p3, w_second, z_out, mixed):
    for p, piece in enumerate((p0, p1, p2, p3)):
        mixed[:, lanes_of(chip(pos) ^ p)] = piece[piece.shape[0] - ROWS :, :]
    z_out[...] = jnp.dot(mixed[...], w_second[...], preferred_element_type=F32).astype(BF16)


def second_layer(pos, pieces, w_second):
    channels = w_second.shape[0]
    return call(
        second_body,
        shaped(ROWS, channels),
        (pos, *pieces, w_second),
        [SMEM] + [VMEM] * 5,
        [pltpu.VMEM((ROWS, channels), BF16)],
    )


def grads_body(pos, mixed, hidden, slope, p0, p1, p2, p3, w_second, keep, send, spread):
    whole_rows(pos, (p0, p1, p2, p3), spread)
    back_hidden = lax.dot_general(
        spread[...],
        w_second[lanes_of(chip(pos)), :],
        (((1,), (1,)), ((), ())),
        preferred_element_type=F32,
    )
    back_first = (back_hidden * slope[...]).astype(BF16)
    over_rows = (((0,), (0,)), ((), ()))
    first = lax.dot_general(mixed[...], back_first, over_rows, preferred_element_type=F32)
    second = lax.dot_general(hidden[...], p0[...], over_rows, preferred_element_type=F32)
    keeps_first = (pos[0] & 1) == 0

    @pl.when(keeps_first)
    def _():
        keep[...] = first
        send[...] = second

    @pl.when(jnp.logical_not(keeps_first))
    def _():
        keep[...] = second
        send[...] = first


def gradients(pos, mixed, hidden, slope, pieces, w_second):
    channels = w_second.shape[0]
    return call(
        grads_body,
        (shaped(channels, LANES, F32), shaped(channels, LANES, F32)),
        (pos, mixed, hidden, slope, *pieces, w_second),
        [SMEM] + [VMEM] * 8,
        [pltpu.VMEM((SPAN, channels), BF16)],
    )


def place_body(pos, *refs):
    mine, other = refs[:QUAD], refs[QUAD : 2 * QUAD]
    outs, staged, sems = refs[2 * QUAD : 2 * QUAD + 2], refs[2 * QUAD + 2 : -1], refs[-1]
    keeps_first = (pos[0] & 1) == 0
    chunk = outs[0].shape[0] // 4
    copies = []
    for i in range(4):
        rows = pl.ds(i * chunk, chunk)

        def fill(mine_out, other_out):
            for p in range(QUAD):
                share = lanes_of(chip(pos) ^ p)
                mine_out[rows, share] = mine[p][rows, :].astype(F32)
                other_out[rows, share] = other[p][rows, :].astype(F32)

        pl.when(keeps_first)(functools.partial(fill, staged[0], staged[1]))
        pl.when(jnp.logical_not(keeps_first))(functools.partial(fill, staged[1], staged[0]))
        for g in range(2):
            copies.append(
                pltpu.make_async_copy(
                    staged[g].at[rows, :], outs[g].at[rows, :], sems.at[2 * i + g]
                )
            )
            copies[-1].start()
    for copy in copies:
        copy.wait()


def place(pos, mine, other):
    channels = QUAD * LANES
    return pl.pallas_call(
        place_body,
        out_shape=(shaped(channels, channels, F32),) * 2,
        in_specs=[SMEM] + [VMEM] * (2 * QUAD),
        out_specs=(HBM, HBM),
        scratch_shapes=[pltpu.VMEM((channels, channels), F32)] * 2
        + [pltpu.SemaphoreType.DMA((8,))],
        compiler_params=PARAMS,
    )(pos, *mine, *other)


def planned_shards(
    features,
    tile_entries,
    tile_columns,
    tiles_per_row,
    rev_vals,
    rev_cols,
    rev_count,
    w_first,
    w_second,
    cotangent,
):
    pos = lax.axis_index(AXES).astype(jnp.int32).reshape(1)
    *packed, tiles, back_tiles = pack(
        pos,
        tile_columns,
        tiles_per_row,
        rev_cols,
        rev_count,
        features,
        cotangent,
        tile_entries,
        rev_vals,
    )
    parts = [packed[0]] + [swap(packed[q], 2 * q) for q in range(1, QUAD)]
    share, places = unpack(pos, parts)
    tiles, back_tiles = join((tiles, swap(tiles, 2), back_tiles, swap(back_tiles, 4)))
    tiles = (tiles, swap(tiles, 4))
    back_tiles = (back_tiles, swap(back_tiles, 2))

    def everywhere(own):
        planes = over_planes(own)
        return planes + [swap(plane, CORE) for plane in planes]

    shares = everywhere(share)
    mixed_share = mix(places, 0, 0, X_THEN_Y, shares, tiles)
    spread_share = mix(places, 2, 1, Y_THEN_X, shares, back_tiles)
    mixed, hidden, hidden_share, slope = first_layer(pos, over_quad(mixed_share), w_first)
    by_one, by_two = swap(hidden_share, 8), swap(hidden_share, 16)
    keep, send = gradients(pos, mixed, hidden, slope, over_quad(spread_share), w_second)
    total = (keep + swap(send, CORE)).astype(BF16)
    across = swap(total, 8)
    total = (total.astype(F32) + across.astype(F32)).astype(BF16)
    by_two, _ = lax.optimization_barrier((by_two, across))
    planes = [hidden_share, by_one, by_two, swap(by_two, 8)]
    total = (total.astype(F32) + swap(total, 16).astype(F32)).astype(BF16)
    planes += [swap(plane, CORE) for plane in planes]
    beside = mix_beside(places, planes, tiles, total)
    mine = [beside[0]] + [swap(beside[q], 2 * q) for q in (3, 2, 1)][::-1]
    z_out = second_layer(pos, mine, w_second)
    grad_first, grad_second = place(pos, mine, [swap(piece, CORE) for piece in mine])
    return (z_out, grad_first, grad_second)


def solution(mesh):
    placed = (
        P(AXES, None),
        P(AXES, None, None),
        P(AXES, None),
        P(AXES),
        P(AXES, None, None),
        P(AXES, None),
        P(AXES),
        P(),
        P(),
        P(AXES, None),
    )
    planned = mesh.shape["rows"] == 8 and mesh.shape["grp"] == 4
    return jax.shard_map(
        planned_shards if planned else gathered_shards,
        mesh=mesh,
        in_specs=placed,
        out_specs=(P(AXES, None), P(), P()),
        check_vma=False,
    )
```
